128 devices in a mesh: tm: 32 (over x, y, core), chan: 4 (over z).
Axes of the slice: x: 4, y: 4, z: 4, core: 2. Of those that a mesh axis runs over, the one named last changes fastest.
Arguments:
- samples: float32 [64, 1048576], P('chan', 'tm'), may hold values from -6 to 6
- start_basis: float32 [512, 128], replicated, may hold values from -6 to 6
Outputs:
- factor: float32 [1024, 1024], P(('tm', 'chan'))
- states: float32 [128, 1048576], P(None, ('tm', 'chan'))
The draws below stay inside these ranges and needn't reach their ends.
All inputs are finite; a program needn't handle non-finite values.
Results may differ from the reference program's by a relative error of at most 0.0003.
Values sent between devices are 32-bit elements; how exact they have to be, the bound alone decides.
No kernel may reach another device: no remote copies, remote signals or barrier semaphores. Data moves between devices by JAX's collectives and lax.ppermute only.
A program may use at most 256 MiB of HBM per device.

```python
import jax
import jax.numpy as jnp
from jax import lax

CH = 64
BR = 16
NS = 128
NSTEPS = 6
ROWS_DEV = 8192
SAMPLES = 1048576
ORDER = 1024


def filtered(noise, ratio):
    taplen = 8
    length = noise.shape[1] - taplen + 1
    result = jnp.zeros((noise.shape[0], length), jnp.float32)
    energy = 0.0
    for j in range(taplen):
        weight = ratio ** j
        energy = energy + weight * weight
        result = result + weight * noise[:, taplen - 1 - j:taplen - 1 - j + length]
    return result * (1.0 / energy ** 0.5)


def draw_samples(key, part):
    taplen = 8
    key_own = jax.random.fold_in(key, 11)
    key_common = jax.random.fold_in(key, 23)
    key_mix = jax.random.fold_in(key, 37)
    own_noise = jax.random.normal(key_own, (CH, SAMPLES + taplen - 1), jnp.float32)
    common_noise = jax.random.normal(key_common, (1, SAMPLES + taplen - 1), jnp.float32)
    mixing = jax.random.uniform(key_mix, (CH, 1), jnp.float32, -0.6, 0.6)
    signal = filtered(own_noise, 0.8) + mixing * filtered(common_noise, -0.7)
    signal = signal * (1.0 / 1.06 ** 0.5)
    return jnp.clip(signal, -6.0, 6.0).astype(jnp.float32)


def centred(rng, dims, width, limit, held_as=jnp.bfloat16):
    values = jax.random.normal(rng, dims, jnp.float32) * width
    return jnp.minimum(jnp.maximum(values, -limit), limit).astype(held_as)


def setup_inputs(seed: int = 0) -> dict:
    key_of = jax.random.split(jax.random.key(seed), 3)
    samples = draw_samples(jax.random.fold_in(key_of[2], 71), 0)
    start_basis = centred(key_of[1], (ORDER // 2, NS), 1.0, 6.0, jnp.float32)
    return dict(samples=samples, start_basis=start_basis)


def windows(padded, start, count):
    segment = lax.dynamic_slice_in_dim(padded, start, count + BR - 1, 1)
    return jnp.concatenate([segment[:, k:k + count] for k in range(BR)], 0)

def reference(samples, start_basis):
    total = samples.shape[1]
    padded = jnp.pad(samples, ((0, 0), (0, BR - 1)))
    blocks = total // ROWS_DEV
    order = BR * CH
    half = order // 2

    def add_block(gram, index):
        slab = windows(padded, (index * ROWS_DEV).astype(jnp.int32), ROWS_DEV)
        first = slab[:CH]
        weight = 1.0 / (1.0 + lax.optimization_barrier(jnp.mean(first * first, 0)))
        term = lax.dot_general((slab * weight[None, :]).astype(jnp.float32), slab.astype(jnp.float32), (((1,), (1,)), ((), ())), precision=lax.Precision.HIGHEST, preferred_element_type=jnp.float32)
        return (gram + term, None)
    gram, _ = lax.scan(add_block, jnp.zeros((order, order), jnp.float32), jnp.arange(blocks, dtype=jnp.int32))
    gram = gram * (1.0 / total)
    factor = jnp.linalg.cholesky(gram).T
    lead = jnp.dot(factor[half:, half:].T.astype(jnp.float32), start_basis.astype(jnp.float32), precision=lax.Precision.HIGHEST, preferred_element_type=jnp.float32)
    basis = lead / jnp.sqrt(jnp.sum(lead * lead))
    for step in range(NSTEPS):
        inner = jnp.dot(basis.T.astype(jnp.float32), basis.astype(jnp.float32), precision=lax.Precision.HIGHEST, preferred_element_type=jnp.float32)
        basis = 1.5 * basis - 0.5 * jnp.dot(basis.astype(jnp.float32), inner.astype(jnp.float32), precision=lax.Precision.HIGHEST, preferred_element_type=jnp.float32)

    def project(index):
        slab = windows(padded, (index * ROWS_DEV).astype(jnp.int32), ROWS_DEV)
        return jnp.dot(basis.T.astype(jnp.float32), slab[half:].astype(jnp.float32), precision=lax.Precision.HIGHEST, preferred_element_type=jnp.float32)
    parts = lax.map(project, jnp.arange(blocks, dtype=jnp.int32))
    states = jnp.transpose(parts, (1, 0, 2)).reshape(basis.shape[1], total)
    return (factor, states)
```

```python
import jax
import jax.numpy as jnp
from jax import lax
from jax.experimental import pallas as pl
from jax.experimental.pallas import tpu as pltpu
from jax.sharding import PartitionSpec as P

BR = 16
NSTEPS = 6
CH = 64
ORDER = 1024
HALF = 512
PANEL = 128
BLOCK = 256
PAD = 128
STEP = 512
TILES = 640
F32 = jnp.float32
BF16 = jnp.bfloat16
EXACT = lax.Precision.HIGHEST
ALL = ("tm", "chan")
NN = (((1,), (0,)), ((), ()))
NT = (((1,), (1,)), ((), ()))
TN = (((0,), (0,)), ((), ()))
VMEM = pl.BlockSpec(memory_space=pltpu.VMEM)
SMEM = pl.BlockSpec(memory_space=pltpu.SMEM)


def params():
    return pltpu.CompilerParams(vmem_limit_bytes=50 << 20)


def mul(left, right, dims, precision=None):
    return lax.dot_general(
        left, right, dims, precision=precision, preferred_element_type=F32
    )


def upper_tiles():
    for top in range(0, ORDER, BLOCK):
        for row in range(top, top + BLOCK, 8):
            for col in range(top, ORDER, 128):
                yield row, col


def split(value):
    high = value.astype(BF16)
    return high, (value - high.astype(F32)).astype(BF16)


def gram_kernel(place_ref, p0_ref, p1_ref, p2_ref, p3_ref, x_ref, packed_ref, h0, l0, h1, l1, g):
    count = x_ref.shape[1] - PAD
    group = CH // 4
    for away, piece in enumerate((p0_ref, p1_ref, p2_ref, p3_ref)):
        owner = (place_ref[0] + 4 - away) % 4
        x_ref[pl.ds(pl.multiple_of(owner * group, group), group), :] = piece[...]

    def prepare(start, high_ref, low_ref):
        window = x_ref[:, pl.ds(start, STEP + PAD)]
        first = window[:, :STEP]
        root = lax.rsqrt(1.0 + jnp.sum(first * first, 0, keepdims=True) * (1.0 / CH))
        for k in range(BR):
            high, low = split(window[:, k : k + STEP] * root)
            high_ref[k * CH : (k + 1) * CH, :] = high
            low_ref[k * CH : (k + 1) * CH, :] = low

    def accumulate(high_ref, low_ref):
        for top in range(0, ORDER, BLOCK):
            rows, cols = slice(top, top + BLOCK), slice(top, ORDER)
            term = mul(high_ref[rows, :], high_ref[cols, :], NT)
            term += mul(high_ref[rows, :], low_ref[cols, :], NT)
            term += mul(low_ref[rows, :], high_ref[cols, :], NT)
            g[rows, cols] += term

    g[...] = jnp.zeros_like(g)
    prepare(0, h0, l0)

    def pair(j, carry):
        base = j * (2 * STEP)
        prepare(pl.multiple_of(base + STEP, STEP), h1, l1)
        accumulate(h0, l0)
        after = jnp.minimum(base + 2 * STEP, count - STEP)
        prepare(pl.multiple_of(after, STEP), h0, l0)
        accumulate(h1, l1)
        return carry

    lax.fori_loop(0, count // (2 * STEP), pair, 0)
    scale = 1.0 / (count * 128)
    for index, (row, col) in enumerate(upper_tiles()):
        piece, at = divmod(index, TILES // 128)
        packed_ref[piece, 8 * at : 8 * at + 8, :] = g[row : row + 8, col : col + 128] * scale


def weighted_gram(place, pieces):
    group, width = pieces[0].shape
    count = width - PAD
    slab = pltpu.VMEM((ORDER, STEP), BF16)
    return pl.pallas_call(
        gram_kernel,
        out_shape=(
            jax.ShapeDtypeStruct((CH, width), F32),
            jax.ShapeDtypeStruct((128, 8 * TILES // 128, 128), F32),
        ),
        in_specs=[SMEM] + [VMEM] * 4,
        out_specs=(VMEM, VMEM),
        scratch_shapes=[slab] * 4 + [pltpu.VMEM((ORDER, ORDER), F32)],
        compiler_params=params(),
        name="gram",
    )(place, *pieces)


def lane(value, j):
    return jnp.broadcast_to(value[:, j : j + 1], (8, 128))


def row(value, j):
    return jnp.broadcast_to(value[j : j + 1, :], (8, 128))


def diagonal_factor(d):
    n = PANEL // 8
    rows = lax.broadcasted_iota(jnp.int32, (8, 128), 0)
    cols = lax.broadcasted_iota(jnp.int32, (8, 128), 1)
    w = [jnp.where(cols == rows + 8 * i, 1.0, 0.0).astype(F32) for i in range(n)]
    upper, inverse = [], []
    for g in range(n):
        cg = [lane(d[g], 8 * g + j) for j in range(8)]
        below = range(g + 1, n)
        cb = {i: [lane(d[i], 8 * g + j) for j in range(8)] for i in below}
        dg, wg = d[g], w[g]
        tops, inv = [], []
        pivots = jnp.zeros((8, 128), F32)
        for j in range(8):
            pivot = row(cg[j], j)
            r = 1.0 / pivot
            inv.append(r)
            pivots = jnp.where(rows == j, pivot, pivots)
            m = jnp.where(rows > j, cg[j] * r, 0.0)
            top = {k: row(cg[k], j) for k in range(j + 1, 8)}
            tops.append(top)
            for k in range(j + 1, 8):
                cg[k] = cg[k] - m * top[k]
            dg = dg - m * row(dg, j)
            wg = wg - m * row(wg, j)
        scale = lax.rsqrt(pivots)
        upper.append(jnp.where(cols >= rows + 8 * g, dg * scale, 0.0))
        inverse.append(wg * scale)
        ds = [row(dg, j) for j in range(8)]
        ws = [row(wg, j) for j in range(8)]
        for i in below:
            c, di, wi = cb[i], d[i], w[i]
            for j in range(8):
                m = c[j] * inv[j]
                for k in range(j + 1, 8):
                    c[k] = c[k] - m * tops[j][k]
                di = di - m * ds[j]
                wi = wi - m * ws[j]
            d[i], w[i] = di, wi
    return upper, inverse


def factor_kernel(place_ref, packed_ref, start_ref, mine_ref, basis_ref, a, u, inverse_ref):
    p = pl.program_id(0)

    @pl.when(p == 0)
    def _():
        u[...] = jnp.zeros_like(u)
        for index, (r, c) in enumerate(upper_tiles()):
            piece, at = divmod(index, TILES // 128)
            a[r : r + 8, c : c + 128] = packed_ref[piece, 8 * at : 8 * at + 8, :]

    o = pl.multiple_of(p * PANEL, PANEL)
    strips = [pl.ds(pl.multiple_of(o + 8 * i, 8), 8) for i in range(PANEL // 8)]
    upper, inverse = diagonal_factor([a[s, pl.ds(o, PANEL)] for s in strips])
    for i, s in enumerate(strips):
        u[s, pl.ds(o, PANEL)] = upper[i]
        inverse_ref[8 * i : 8 * i + 8, :] = inverse[i]
    for q in range(ORDER // PANEL - 1):

        @pl.when(p == q)
        def _():
            top, s = q * PANEL, (q + 1) * PANEL
            panel = mul(inverse_ref[...], a[top:s, s:], NN, EXACT)
            u[top:s, s:] = panel
            for b in range(s, ORDER, BLOCK):
                e = min(b + BLOCK, ORDER)
                a[b:e, b:] -= mul(panel[:, b - s : e - s], panel[:, b - s :], TN, EXACT)

    @pl.when(p == ORDER // PANEL - 1)
    def _():
        share = mine_ref.shape[0]
        mine_ref[...] = u[pl.ds(pl.multiple_of(place_ref[0] * share, share), share), :]
        lead = mul(start_ref[...], u[HALF:, HALF:], TN, EXACT)
        basis = lead / jnp.sqrt(jnp.sum(lead * lead))
        inner = mul(basis, basis, NT, EXACT)
        states = inner.shape[0]
        eye = jnp.where(
            lax.broadcasted_iota(jnp.int32, (states, states), 0)
            == lax.broadcasted_iota(jnp.int32, (states, states), 1),
            1.5,
            0.0,
        ).astype(F32)
        total = None
        for step in range(NSTEPS):
            m = eye - 0.5 * inner
            total = m if total is None else mul(total, m, NN, EXACT)
            if step < NSTEPS - 1:
                inner = mul(mul(inner, m, NN, EXACT), m, NN, EXACT)
        basis_ref[...] = mul(total, basis, NN, EXACT)


def factor_and_basis(place, packed, start, share):
    whole = lambda shape: pl.BlockSpec(shape, lambda i: (0,) * len(shape))
    states = start.shape[1]
    return pl.pallas_call(
        factor_kernel,
        grid=(ORDER // PANEL,),
        out_shape=(
            jax.ShapeDtypeStruct((share, ORDER), F32),
            jax.ShapeDtypeStruct((states, HALF), F32),
        ),
        in_specs=[SMEM, whole(packed.shape), whole(start.shape)],
        out_specs=(whole((share, ORDER)), whole((states, HALF))),
        scratch_shapes=[
            pltpu.VMEM((ORDER, ORDER), F32),
            pltpu.VMEM((ORDER, ORDER), F32),
            pltpu.VMEM((PANEL, PANEL), F32),
        ],
        compiler_params=params(),
        name="factor",
    )(place, packed, start)


def states_kernel(basis_ref, x_ref, out_ref, high_ref, low_ref):
    span = out_ref.shape[1]
    start = pl.multiple_of(pl.program_id(0) * span, span)
    window = x_ref[:, pl.ds(start, span + PAD)]
    first = BR // 2
    for k in range(first):
        high, low = split(window[:, first + k : first + k + span])
        high_ref[k * CH : (k + 1) * CH, :] = high
        low_ref[k * CH : (k + 1) * CH, :] = low
    bh, bl = split(basis_ref[...])
    out = mul(bh, high_ref[...], NN)
    out += mul(bl, high_ref[...], NN)
    out_ref[...] = out + mul(bh, low_ref[...], NN)


def project(basis, x):
    states = basis.shape[0]
    count = x.shape[1] - PAD
    span = 1024
    slab = pltpu.VMEM((HALF, span), BF16)
    return pl.pallas_call(
        states_kernel,
        grid=(count // span,),
        out_shape=jax.ShapeDtypeStruct((states, count), F32),
        in_specs=[
            pl.BlockSpec(basis.shape, lambda i: (0, 0)),
            pl.BlockSpec(x.shape, lambda i: (0, 0)),
        ],
        out_specs=pl.BlockSpec((states, span), lambda i: (0, i)),
        scratch_shapes=[slab, slab],
        compiler_params=params(),
        name="states",
    )(basis, x)


def per_device(samples, start_basis):
    tms, chans = lax.axis_size("tm"), lax.axis_size("chan")
    count = samples.shape[1] // chans
    chan = lax.axis_index("chan")
    halo = lax.ppermute(samples[:, :PAD], "tm", [(i, i - 1) for i in range(1, tms)])
    extended = jnp.concatenate([samples, halo], 1)
    pieces = []
    for away in range(chans):
        to = (chan + away) % chans
        window = lax.dynamic_slice_in_dim(extended, to * count, count + PAD, 1)
        if away:
            window = lax.ppermute(window, "chan", [(i, (i + away) % chans) for i in range(chans)])
        pieces.append(window)
    x, packed = weighted_gram(chan[None].astype(jnp.int32), pieces)
    packed = lax.all_to_all(packed, ALL, 0, 0, tiled=True)
    total = jnp.sum(packed, 0)
    packed = jnp.broadcast_to(total[None], packed.shape)
    packed = lax.all_to_all(packed, ALL, 0, 0, tiled=True)
    position = lax.axis_index(ALL)[None].astype(jnp.int32)
    mine, basis = factor_and_basis(position, packed, start_basis, ORDER // (tms * chans))
    return (mine, project(basis, x))


def solution(mesh):
    return jax.shard_map(
        per_device,
        mesh=mesh,
        in_specs=(P("chan", "tm"), P()),
        out_specs=(P(ALL, None), P(None, ALL)),
        check_vma=False,
    )
```

```python
import functools

import jax
import jax.numpy as jnp
from jax import lax
from jax.experimental import pallas as pl
from jax.experimental.pallas import tpu as pltpu
from jax.sharding import Mesh
from jax.sharding import PartitionSpec as P

BR = 16
NSTEPS = 6
CH = 64
ORDER = 1024
HALF = 512
PANEL = 128
BLOCK = 256
PAD = 128
STEP = 512
CHUNK = 3072
TILES = 640
F32 = jnp.float32
BF16 = jnp.bfloat16
EXACT = lax.Precision.HIGHEST
ALL = ("x", "y", "core", "chan")
TIME = ("x", "y", "core")
CHIPS = ("x", "y", "chan")
NN = (((1,), (0,)), ((), ()))
NT = (((1,), (1,)), ((), ()))
TN = (((0,), (0,)), ((), ()))
VMEM = pl.BlockSpec(memory_space=pltpu.VMEM)
SMEM = pl.BlockSpec(memory_space=pltpu.SMEM)


def params(mebibytes):
    return pltpu.CompilerParams(vmem_limit_bytes=mebibytes << 20)


def mul(left, right, dims, precision=None):
    return lax.dot_general(
        left, right, dims, precision=precision, preferred_element_type=F32
    )


def upper_tiles():
    for top in range(0, ORDER, BLOCK):
        for row in range(top, top + BLOCK, 8):
            for col in range(top, ORDER, 128):
                yield row, col


def split(value):
    high = value.astype(BF16)
    return high, (value - high.astype(F32)).astype(BF16)


def gram_kernel(size, start, place_ref, p0_ref, p1_ref, p2_ref, p3_ref, *refs):
    if start is None:
        x_ref, out_ref, h0, l0, h1, l1, g, cross = refs
        base = 0
    else:
        before_ref, sofar_ref, x_ref, keep_ref, send_ref, h0, l0, h1, l1, g, cross = refs
        base = start
        x_ref[:, :start] = before_ref[:, :start]
    group = CH // 4
    for away, piece in enumerate((p0_ref, p1_ref, p2_ref, p3_ref)):
        owner = (place_ref[0] + 4 - away) % 4
        x_ref[pl.ds(pl.multiple_of(owner * group, group), group), base:] = piece[...]

    def prepare(at, high_ref, low_ref):
        window = x_ref[:, pl.ds(at, STEP + PAD)]
        first = window[:, :STEP]
        root = lax.rsqrt(1.0 + jnp.sum(first * first, 0, keepdims=True) * (1.0 / CH))
        for k in range(BR):
            high, low = split(window[:, k : k + STEP] * root)
            high_ref[k * CH : (k + 1) * CH, :] = high
            low_ref[k * CH : (k + 1) * CH, :] = low

    def accumulate(high_ref, low_ref):
        for index, top in enumerate(range(0, ORDER, BLOCK)):
            end = top + BLOCK
            rows, cols = slice(top, end), slice(top, ORDER)
            both = mul(high_ref[rows, :], high_ref[cols, :], NT)
            mixed = mul(high_ref[rows, :], low_ref[cols, :], NT)
            g[rows, rows] += both[:, :BLOCK]
            cross[index] += mixed[:, :BLOCK]
            if end < ORDER:
                rest = slice(end, ORDER)
                other = mul(low_ref[rows, :], high_ref[rest, :], NT)
                g[rows, rest] += both[:, BLOCK:] + mixed[:, BLOCK:] + other

    g[...] = jnp.zeros_like(g) if start is None else sofar_ref[...]
    cross[...] = jnp.zeros_like(cross)
    prepare(base, h0, l0)

    def pair(j, carry):
        at = base + j * (2 * STEP)
        prepare(pl.multiple_of(at + STEP, STEP), h1, l1)
        accumulate(h0, l0)
        after = jnp.minimum(at + 2 * STEP, base + size - STEP)
        prepare(pl.multiple_of(after, STEP), h0, l0)
        accumulate(h1, l1)
        return carry

    lax.fori_loop(0, size // (2 * STEP), pair, 0)
    for index, top in enumerate(range(0, ORDER, BLOCK)):
        rows = slice(top, top + BLOCK)
        g[rows, rows] += cross[index] + cross[index].T
    if start is None:
        out_ref[...] = g[...]
        return
    scale = 1.0 / ((base + size) * 128)
    for core in range(2):

        @pl.when(place_ref[1] == core)
        def _():
            for tile, (row, col) in enumerate(upper_tiles()):
                half, piece, at = where(tile)
                to_ref = keep_ref if half == core else send_ref
                to_ref[piece, at : at + 8, :] = g[row : row + 8, col : col + 128] * scale


def where(tile):
    piece, at = divmod(tile, TILES // 128)
    return piece // 64, piece % 64, 8 * at


def gram_chunk(place, pieces, before=None):
    group, width = pieces[0].shape
    size = width - PAD
    slab = pltpu.VMEM((ORDER, STEP), BF16)
    gram = jax.ShapeDtypeStruct((ORDER, ORDER), F32)
    half = jax.ShapeDtypeStruct((64, 8 * TILES // 128, 128), F32)
    start = None if before is None else before[0].shape[1] - PAD
    given = [] if before is None else list(before)
    x = jax.ShapeDtypeStruct((CH, width + (start or 0)), F32)
    out = (x, gram) if start is None else (x, half, half)
    return pl.pallas_call(
        functools.partial(gram_kernel, size, start),
        out_shape=out,
        in_specs=[SMEM] + [VMEM] * (4 + len(given)),
        out_specs=(VMEM,) * len(out),
        scratch_shapes=[slab] * 4
        + [pltpu.VMEM((ORDER, ORDER), F32), pltpu.VMEM((ORDER // BLOCK, BLOCK, BLOCK), F32)],
        compiler_params=params(32),
        name="gram_first" if start is None else "gram_last",
    )(place, *pieces, *given)


def lane(value, j):
    return jnp.broadcast_to(value[:, j : j + 1], (8, 128))


def row(value, j):
    return jnp.broadcast_to(value[j : j + 1, :], (8, 128))


def diagonal_factor(d):
    n = PANEL // 8
    rows = lax.broadcasted_iota(jnp.int32, (8, 128), 0)
    cols = lax.broadcasted_iota(jnp.int32, (8, 128), 1)
    w = [jnp.where(cols == rows + 8 * i, 1.0, 0.0).astype(F32) for i in range(n)]
    upper, inverse = [], []
    for g in range(n):
        cg = [lane(d[g], 8 * g + j) for j in range(8)]
        below = range(g + 1, n)
        cb = {i: [lane(d[i], 8 * g + j) for j in range(8)] for i in below}
        dg, wg = d[g], w[g]
        tops, inv = [], []
        pivots = jnp.zeros((8, 128), F32)
        for j in range(8):
            pivot = row(cg[j], j)
            r = 1.0 / pivot
            inv.append(r)
            pivots = jnp.where(rows == j, pivot, pivots)
            m = jnp.where(rows > j, cg[j] * r, 0.0)
            top = {k: row(cg[k], j) for k in range(j + 1, 8)}
            tops.append(top)
            for k in range(j + 1, 8):
                cg[k] = cg[k] - m * top[k]
            dg = dg - m * row(dg, j)
            wg = wg - m * row(wg, j)
        scale = lax.rsqrt(pivots)
        upper.append(jnp.where(cols >= rows + 8 * g, dg * scale, 0.0))
        inverse.append(wg * scale)
        ds = [row(dg, j) for j in range(8)]
        ws = [row(wg, j) for j in range(8)]
        for i in below:
            c, di, wi = cb[i], d[i], w[i]
            for j in range(8):
                m = c[j] * inv[j]
                for k in range(j + 1, 8):
                    c[k] = c[k] - m * tops[j][k]
                di = di - m * ds[j]
                wi = wi - m * ws[j]
            d[i], w[i] = di, wi
    return upper, inverse


def factor_kernel(place_ref, own_ref, other_ref, start_ref, mine_ref, basis_ref, a, u, inverse_ref):
    p = pl.program_id(0)

    @pl.when(p == 0)
    def _():
        u[...] = jnp.zeros_like(u)
        for core in range(2):

            @pl.when(place_ref[1] == core)
            def _():
                for tile, (r, c) in enumerate(upper_tiles()):
                    half, piece, at = where(tile)
                    from_ref = own_ref if half == core else other_ref
                    a[r : r + 8, c : c + 128] = from_ref[piece, at : at + 8, :]

    o = pl.multiple_of(p * PANEL, PANEL)
    strips = [pl.ds(pl.multiple_of(o + 8 * i, 8), 8) for i in range(PANEL // 8)]
    upper, inverse = diagonal_factor([a[s, pl.ds(o, PANEL)] for s in strips])
    for i, s in enumerate(strips):
        u[s, pl.ds(o, PANEL)] = upper[i]
        inverse_ref[8 * i : 8 * i + 8, :] = inverse[i]
    for q in range(ORDER // PANEL - 1):

        @pl.when(p == q)
        def _():
            top, s = q * PANEL, (q + 1) * PANEL
            panel = mul(inverse_ref[...], a[top:s, s:], NN, EXACT)
            u[top:s, s:] = panel
            for b in range(s, ORDER, BLOCK):
                e = min(b + BLOCK, ORDER)
                a[b:e, b:] -= mul(panel[:, b - s : e - s], panel[:, b - s :], TN, EXACT)

    @pl.when(p == ORDER // PANEL - 1)
    def _():
        share = mine_ref.shape[0]
        mine_ref[...] = u[pl.ds(pl.multiple_of(place_ref[0] * share, share), share), :]
        lead = mul(start_ref[...], u[HALF:, HALF:], TN, EXACT)
        basis = lead / jnp.sqrt(jnp.sum(lead * lead))
        inner = mul(basis, basis, NT, EXACT)
        states = inner.shape[0]
        eye = jnp.where(
            lax.broadcasted_iota(jnp.int32, (states, states), 0)
            == lax.broadcasted_iota(jnp.int32, (states, states), 1),
            1.5,
            0.0,
        ).astype(F32)
        total = None
        for step in range(NSTEPS):
            m = eye - 0.5 * inner
            total = m if total is None else mul(total, m, NN, EXACT)
            if step < NSTEPS - 1:
                inner = mul(mul(inner, m, NN, EXACT), m, NN, EXACT)
        basis_ref[...] = mul(total, basis, NN, EXACT)


def factor_and_basis(place, own, other, start, share):
    whole = lambda shape: pl.BlockSpec(shape, lambda i: (0,) * len(shape))
    states = start.shape[1]
    return pl.pallas_call(
        factor_kernel,
        grid=(ORDER // PANEL,),
        out_shape=(
            jax.ShapeDtypeStruct((share, ORDER), F32),
            jax.ShapeDtypeStruct((states, HALF), F32),
        ),
        in_specs=[SMEM, whole(own.shape), whole(other.shape), whole(start.shape)],
        out_specs=(whole((share, ORDER)), whole((states, HALF))),
        scratch_shapes=[
            pltpu.VMEM((ORDER, ORDER), F32),
            pltpu.VMEM((ORDER, ORDER), F32),
            pltpu.VMEM((PANEL, PANEL), F32),
        ],
        compiler_params=params(32),
        name="factor",
    )(place, own, other, start)


def states_kernel(basis_ref, x_ref, out_ref, high_ref, low_ref):
    span = out_ref.shape[1]
    start = pl.multiple_of(pl.program_id(0) * span, span)
    window = x_ref[:, pl.ds(start, span + PAD)]
    first = BR // 2
    for k in range(first):
        high, low = split(window[:, first + k : first + k + span])
        high_ref[k * CH : (k + 1) * CH, :] = high
        low_ref[k * CH : (k + 1) * CH, :] = low
    bh, bl = split(basis_ref[...])
    out = mul(bh, high_ref[...], NN)
    out += mul(bl, high_ref[...], NN)
    out_ref[...] = out + mul(bh, low_ref[...], NN)


def project(basis, x):
    states = basis.shape[0]
    count = x.shape[1] - PAD
    span = 1024
    slab = pltpu.VMEM((HALF, span), BF16)
    return pl.pallas_call(
        states_kernel,
        grid=(count // span,),
        out_shape=jax.ShapeDtypeStruct((states, count), F32),
        in_specs=[
            pl.BlockSpec(basis.shape, lambda i: (0, 0)),
            pl.BlockSpec(x.shape, lambda i: (0, 0)),
        ],
        out_specs=pl.BlockSpec((states, span), lambda i: (0, i)),
        scratch_shapes=[slab, slab],
        compiler_params=params(32),
        name="states",
    )(basis, x)


def from_chans(array, starts, width):
    chans = lax.axis_size("chan")
    chan = lax.axis_index("chan")
    pieces = []
    for away in range(chans):
        window = lax.dynamic_slice_in_dim(array, starts((chan + away) % chans), width, 1)
        if away:
            window = lax.ppermute(window, "chan", [(i, (i + away) % chans) for i in range(chans)])
        pieces.append(window)
    return pieces


def per_device(samples, start_basis):
    times, chans = lax.axis_size(TIME), lax.axis_size("chan")
    count = samples.shape[1] // chans
    core = lax.axis_index("core")
    place = jnp.stack([lax.axis_index("chan"), core]).astype(jnp.int32)
    halo = lax.ppermute(samples[:, :PAD], TIME, [(i, i - 1) for i in range(1, times)])
    pieces = from_chans(samples, lambda to: to * count, CHUNK + PAD)
    extended = jnp.concatenate([samples, halo], 1)
    pieces, extended = lax.optimization_barrier((pieces, extended))
    others = from_chans(extended, lambda to: to * count + CHUNK, count - CHUNK + PAD)
    first, sofar = gram_chunk(place, pieces)
    x, keep, send = gram_chunk(place, others, (first, sofar))
    swap = [(0, 1), (1, 0)]
    half = keep + lax.ppermute(send, "core", swap)
    half = lax.all_to_all(half, CHIPS, 0, 0, tiled=True)
    half = jnp.broadcast_to(jnp.sum(half, 0)[None], half.shape)
    half = lax.all_to_all(half, CHIPS, 0, 0, tiled=True)
    other = lax.ppermute(half, "core", swap)
    place = jnp.stack([lax.axis_index(ALL), core]).astype(jnp.int32)
    mine, basis = factor_and_basis(place, half, other, start_basis, ORDER // (times * chans))
    return (mine, project(basis, x))


def solution(mesh):
    mesh = Mesh(mesh.devices.reshape(4, 4, 2, 4), ALL)
    return jax.shard_map(
        per_device,
        mesh=mesh,
        in_specs=(P("chan", TIME), P()),
        out_specs=(P(ALL, None), P(None, ALL)),
        check_vma=False,
    )
```

```python
import functools

import jax
import jax.numpy as jnp
from jax import lax
from jax.experimental import pallas as pl
from jax.experimental.pallas import tpu as pltpu
from jax.sharding import Mesh
from jax.sharding import PartitionSpec as P

BR = 16
NSTEPS = 6
CH = 64
ORDER = 1024
HALF = 512
PANEL = 128
BLOCK = 256
PAD = 128
STEP = 512
CHUNK = 3072
TILES = 640
F32 = jnp.float32
BF16 = jnp.bfloat16
EXACT = lax.Precision.HIGHEST
ALL = ("x", "y", "core", "chan")
TIME = ("x", "y", "core")
CHIPS = ("x", "y", "chan")
NN = (((1,), (0,)), ((), ()))
NT = (((1,), (1,)), ((), ()))
TN = (((0,), (0,)), ((), ()))
VMEM = pl.BlockSpec(memory_space=pltpu.VMEM)
SMEM = pl.BlockSpec(memory_space=pltpu.SMEM)
HBM = pl.BlockSpec(memory_space=pltpu.HBM)


def params(mebibytes):
    return pltpu.CompilerParams(vmem_limit_bytes=mebibytes << 20)


def mul(left, right, dims, precision=None):
    return lax.dot_general(
        left, right, dims, precision=precision, preferred_element_type=F32
    )


def upper_tiles():
    for top in range(0, ORDER, BLOCK):
        for row in range(top, top + BLOCK, 8):
            for col in range(top, ORDER, 128):
                yield row, col


def split(value):
    high = value.astype(BF16)
    return high, (value - high.astype(F32)).astype(BF16)


def gram_kernel(size, start, place_ref, p0_ref, p1_ref, p2_ref, p3_ref, *refs):
    if start is None:
        x_ref, g, h0, l0, h1, l1, cross, sems = refs
        base = 0
        first = pl.multiple_of(place_ref[0] * (p0_ref.shape[1] // 4), 128)
        p0_ref = p0_ref.at[:, pl.ds(first, size + PAD)]
    else:
        before_ref, sofar_ref, x_ref, keep_ref, send_ref, h0, l0, h1, l1, g, cross, sems = refs
        base = start
    group = CH // 4
    copies = []
    for away, piece in enumerate((p0_ref, p1_ref, p2_ref, p3_ref)):
        owner = (place_ref[0] + 4 - away) % 4
        to = x_ref.at[pl.ds(pl.multiple_of(owner * group, group), group), pl.ds(base, size + PAD)]
        copies.append(pltpu.make_async_copy(piece, to, sems.at[away]))
    for copy in copies:
        copy.start()

    def prepare(at, high_ref, low_ref):
        window = x_ref[:, pl.ds(at, STEP + PAD)]
        first = window[:, :STEP]
        root = lax.rsqrt(1.0 + jnp.sum(first * first, 0, keepdims=True) * (1.0 / CH))
        for k in range(BR):
            high, low = split(window[:, k : k + STEP] * root)
            high_ref[k * CH : (k + 1) * CH, :] = high
            low_ref[k * CH : (k + 1) * CH, :] = low

    def accumulate(high_ref, low_ref):
        for index, top in enumerate(range(0, ORDER, BLOCK)):
            end = top + BLOCK
            rows, cols = slice(top, end), slice(top, ORDER)
            both = mul(high_ref[rows, :], high_ref[cols, :], NT)
            mixed = mul(high_ref[rows, :], low_ref[cols, :], NT)
            g[rows, rows] += both[:, :BLOCK]
            cross[index] += mixed[:, :BLOCK]
            if end < ORDER:
                rest = slice(end, ORDER)
                other = mul(low_ref[rows, :], high_ref[rest, :], NT)
                g[rows, rest] += both[:, BLOCK:] + mixed[:, BLOCK:] + other

    cross[...] = jnp.zeros_like(cross)
    if start is None:
        g[...] = jnp.zeros_like(g)
    else:
        g[...] = sofar_ref[...]
        x_ref[:, :start] = before_ref[:, :start]
    for copy in copies:
        copy.wait()
    prepare(base, h0, l0)

    def pair(j, carry):
        at = base + j * (2 * STEP)
        prepare(pl.multiple_of(at + STEP, STEP), h1, l1)
        accumulate(h0, l0)
        after = jnp.minimum(at + 2 * STEP, base + size - STEP)
        prepare(pl.multiple_of(after, STEP), h0, l0)
        accumulate(h1, l1)
        return carry

    lax.fori_loop(0, size // (2 * STEP), pair, 0)
    for index, top in enumerate(range(0, ORDER, BLOCK)):
        rows = slice(top, top + BLOCK)
        g[rows, rows] += cross[index] + cross[index].T
    if start is None:
        return
    scale = 1.0 / ((base + size) * 128)
    for core in range(2):

        @pl.when(place_ref[1] == core)
        def _():
            for tile, (row, col) in enumerate(upper_tiles()):
                half, piece, at = where(tile)
                to_ref = keep_ref if half == core else send_ref
                to_ref[piece, at : at + 8, :] = g[row : row + 8, col : col + 128] * scale


def where(tile):
    piece, at = divmod(tile, TILES // 128)
    return piece // 64, piece % 64, 8 * at


def gram_chunk(place, pieces, before=None):
    size = pieces[1].shape[1] - PAD
    slab = pltpu.VMEM((ORDER, STEP), BF16)
    gram = jax.ShapeDtypeStruct((ORDER, ORDER), F32)
    half = jax.ShapeDtypeStruct((64, 8 * TILES // 128, 128), F32)
    start = None if before is None else before[0].shape[1] - PAD
    given = [] if before is None else list(before)
    pieces = [pltpu.with_memory_space_constraint(piece, pltpu.HBM) for piece in pieces]
    x = jax.ShapeDtypeStruct((CH, size + PAD + (start or 0)), F32)
    out = (x, gram) if start is None else (x, half, half)
    return pl.pallas_call(
        functools.partial(gram_kernel, size, start),
        out_shape=out,
        in_specs=[SMEM] + [HBM] * 4 + [VMEM] * len(given),
        out_specs=(VMEM,) * len(out),
        scratch_shapes=[slab] * 4
        + ([] if start is None else [pltpu.VMEM((ORDER, ORDER), F32)])
        + [pltpu.VMEM((ORDER // BLOCK, BLOCK, BLOCK), F32), pltpu.SemaphoreType.DMA((4,))],
        compiler_params=params(32),
        name="gram_first" if start is None else "gram_last",
    )(place, *pieces, *given)


def lane(value, j):
    return jnp.broadcast_to(value[:, j : j + 1], (8, 128))


def row(value, j):
    return jnp.broadcast_to(value[j : j + 1, :], (8, 128))


def diagonal_factor(d):
    n = PANEL // 8
    rows = lax.broadcasted_iota(jnp.int32, (8, 128), 0)
    cols = lax.broadcasted_iota(jnp.int32, (8, 128), 1)
    w = [jnp.where(cols == rows + 8 * i, 1.0, 0.0).astype(F32) for i in range(n)]
    upper, inverse = [], []
    for g in range(n):
        cg = [lane(d[g], 8 * g + j) for j in range(8)]
        below = range(g + 1, n)
        cb = {i: [lane(d[i], 8 * g + j) for j in range(8)] for i in below}
        dg, wg = d[g], w[g]
        tops, inv = [], []
        pivots = jnp.zeros((8, 128), F32)
        for j in range(8):
            pivot = row(cg[j], j)
            r = 1.0 / pivot
            inv.append(r)
            pivots = jnp.where(rows == j, pivot, pivots)
            m = jnp.where(rows > j, cg[j] * r, 0.0)
            top = {k: row(cg[k], j) for k in range(j + 1, 8)}
            tops.append(top)
            for k in range(j + 1, 8):
                cg[k] = cg[k] - m * top[k]
            dg = dg - m * row(dg, j)
            wg = wg - m * row(wg, j)
        scale = lax.rsqrt(pivots)
        upper.append(jnp.where(cols >= rows + 8 * g, dg * scale, 0.0))
        inverse.append(wg * scale)
        ds = [row(dg, j) for j in range(8)]
        ws = [row(wg, j) for j in range(8)]
        for i in below:
            c, di, wi = cb[i], d[i], w[i]
            for j in range(8):
                m = c[j] * inv[j]
                for k in range(j + 1, 8):
                    c[k] = c[k] - m * tops[j][k]
                di = di - m * ds[j]
                wi = wi - m * ws[j]
            d[i], w[i] = di, wi
    return upper, inverse


def factor_kernel(
    place_ref, own_ref, other_ref, given_ref, mine_ref, basis_ref, a, u, inverse_ref, start_ref, sem
):
    p = pl.program_id(0)
    last = ORDER // PANEL - 1
    fetch = pltpu.make_async_copy(given_ref, start_ref, sem.at[0])

    @pl.when(p == 0)
    def _():
        fetch.start()
        for core in range(2):

            @pl.when(place_ref[1] == core)
            def _():
                for tile, (r, c) in enumerate(upper_tiles()):
                    half, piece, at = where(tile)
                    from_ref = own_ref if half == core else other_ref
                    a[r : r + 8, c : c + 128] = from_ref[piece, at : at + 8, :]

    o = pl.multiple_of(p * PANEL, PANEL)
    strips = [pl.ds(pl.multiple_of(o + 8 * i, 8), 8) for i in range(PANEL // 8)]
    upper, inverse = diagonal_factor([a[s, pl.ds(o, PANEL)] for s in strips])
    for i, s in enumerate(strips):
        u[s, pl.ds(o, PANEL)] = upper[i]
        inverse_ref[8 * i : 8 * i + 8, :] = inverse[i]
    for q in range(ORDER // PANEL - 1):

        @pl.when(p == q)
        def _():
            top, s = q * PANEL, (q + 1) * PANEL
            panel = mul(inverse_ref[...], a[top:s, s:], NN, EXACT)
            u[top:s, s:] = panel
            high, low = split(panel)
            for b in range(s, ORDER, BLOCK):
                rows, cols = slice(b - s, min(b + BLOCK, ORDER) - s), slice(b - s, ORDER - s)
                term = mul(high[:, rows], high[:, cols], TN)
                term += mul(high[:, rows], low[:, cols], TN)
                a[b : b + BLOCK, b:] -= term + mul(low[:, rows], high[:, cols], TN)

    @pl.when(p == last)
    def _():
        share = mine_ref.shape[0]
        top = pl.multiple_of(place_ref[0] * share, share)
        below = lax.broadcasted_iota(jnp.int32, mine_ref.shape, 0) + top
        cols = lax.broadcasted_iota(jnp.int32, mine_ref.shape, 1)
        mine_ref[...] = jnp.where(cols >= below, u[pl.ds(top, share), :], 0.0)
        for q in range(HALF // PANEL, last):
            s = (q + 1) * PANEL
            u[s:, q * PANEL : s] = jnp.zeros((ORDER - s, PANEL), F32)
        fetch.wait()
        lead = mul(start_ref[...], u[HALF:, HALF:], TN, EXACT)
        basis = lead / jnp.sqrt(jnp.sum(lead * lead))
        inner = mul(basis, basis, NT, EXACT)
        states = inner.shape[0]
        eye = jnp.where(
            lax.broadcasted_iota(jnp.int32, (states, states), 0)
            == lax.broadcasted_iota(jnp.int32, (states, states), 1),
            1.5,
            0.0,
        ).astype(F32)
        total = None
        for step in range(NSTEPS):
            m = eye - 0.5 * inner
            total = m if total is None else mul(total, m, NN, EXACT)
            if step < NSTEPS - 1:
                inner = mul(mul(inner, m, NN, EXACT), m, NN, EXACT)
        basis_ref[...] = mul(total, basis, NN, EXACT)


def factor_and_basis(place, own, other, start, share):
    whole = lambda shape: pl.BlockSpec(shape, lambda i: (0,) * len(shape))
    states = start.shape[1]
    return pl.pallas_call(
        factor_kernel,
        grid=(ORDER // PANEL,),
        out_shape=(
            jax.ShapeDtypeStruct((share, ORDER), F32),
            jax.ShapeDtypeStruct((states, HALF), F32),
        ),
        in_specs=[SMEM, whole(own.shape), whole(other.shape), HBM],
        out_specs=(whole((share, ORDER)), whole((states, HALF))),
        scratch_shapes=[
            pltpu.VMEM((ORDER, ORDER), F32),
            pltpu.VMEM((ORDER, ORDER), F32),
            pltpu.VMEM((PANEL, PANEL), F32),
            pltpu.VMEM(start.shape, F32),
            pltpu.SemaphoreType.DMA((1,)),
        ],
        compiler_params=params(32),
        name="factor",
    )(place, own, other, pltpu.with_memory_space_constraint(start, pltpu.HBM))


def states_kernel(basis_ref, x_ref, out_ref, high_ref, low_ref):
    span = out_ref.shape[1]
    start = pl.multiple_of(pl.program_id(0) * span, span)
    window = x_ref[:, pl.ds(start, span + PAD)]
    first = BR // 2
    for k in range(first):
        high, low = split(window[:, first + k : first + k + span])
        high_ref[k * CH : (k + 1) * CH, :] = high
        low_ref[k * CH : (k + 1) * CH, :] = low
    bh, bl = split(basis_ref[...])
    out = mul(bh, high_ref[...], NN)
    out += mul(bl, high_ref[...], NN)
    out_ref[...] = out + mul(bh, low_ref[...], NN)


def project(basis, x):
    states = basis.shape[0]
    count = x.shape[1] - PAD
    span = 2048
    slab = pltpu.VMEM((HALF, span), BF16)
    return pl.pallas_call(
        states_kernel,
        grid=(count // span,),
        out_shape=jax.ShapeDtypeStruct((states, count), F32),
        in_specs=[
            pl.BlockSpec(basis.shape, lambda i: (0, 0)),
            pl.BlockSpec(x.shape, lambda i: (0, 0)),
        ],
        out_specs=pl.BlockSpec((states, span), lambda i: (0, i)),
        scratch_shapes=[slab, slab],
        compiler_params=params(32),
        name="states",
    )(basis, x)


def windows(array, starts, width, nearest):
    chans, chan = lax.axis_size("chan"), lax.axis_index("chan")
    return [
        lax.dynamic_slice_in_dim(array, starts((chan + away) % chans), width, 1)
        for away in range(nearest, chans)
    ]


def exchange(owed):
    chans = lax.axis_size("chan")
    return [
        lax.ppermute(window, "chan", [(i, (i + away) % chans) for i in range(chans)])
        for away, window in enumerate(owed, 1)
    ]


def per_device(samples, start_basis):
    times, chans = lax.axis_size(TIME), lax.axis_size("chan")
    count = samples.shape[1] // chans
    core = lax.axis_index("core")
    place = jnp.stack([lax.axis_index("chan"), core]).astype(jnp.int32)
    owed = windows(samples, lambda to: to * count, CHUNK + PAD, 1)
    owed, head = lax.optimization_barrier((owed, samples[:, :PAD]))
    arrived = exchange(owed)
    halo = lax.ppermute(head, TIME, [(i, i - 1) for i in range(1, times)])
    extended = jnp.concatenate([samples, halo], 1)
    arrived, extended = lax.optimization_barrier((arrived, extended))
    own, *owed = windows(extended, lambda to: to * count + CHUNK, count - CHUNK + PAD, 0)
    others = [own] + exchange(owed)
    first, sofar = gram_chunk(place, [samples] + arrived)
    x, keep, send = gram_chunk(place, others, (first, sofar))
    swap = [(0, 1), (1, 0)]
    half = keep + lax.ppermute(send, "core", swap)
    half = lax.all_to_all(half, CHIPS, 0, 0, tiled=True)
    half = jnp.broadcast_to(jnp.sum(half, 0)[None], half.shape)
    half = lax.all_to_all(half, CHIPS, 0, 0, tiled=True)
    other = lax.ppermute(half, "core", swap)
    place = jnp.stack([lax.axis_index(ALL), core]).astype(jnp.int32)
    mine, basis = factor_and_basis(place, half, other, start_basis, ORDER // (times * chans))
    return (mine, project(basis, x))


def solution(mesh):
    mesh = Mesh(mesh.devices.reshape(4, 4, 2, 4), ALL)
    return jax.shard_map(
        per_device,
        mesh=mesh,
        in_specs=(P("chan", TIME), P()),
        out_specs=(P(ALL, None), P(None, ALL)),
        check_vma=False,
    )
```

```python
import functools

import jax
import jax.numpy as jnp
from jax import lax
from jax.experimental import pallas as pl
from jax.experimental.pallas import tpu as pltpu
from jax.sharding import Mesh
from jax.sharding import PartitionSpec as P

BR = 16
NSTEPS = 6
CH = 64
ORDER = 1024
HALF = 512
PANEL = 128
BLOCK = 256
PAD = 128
STEP = 512
CHUNK = 2048
EARLY = 1664
TILES = 640
F32 = jnp.float32
BF16 = jnp.bfloat16
EXACT = lax.Precision.HIGHEST
ALL = ("x", "y", "core", "chan")
TIME = ("x", "y", "core")
CHIPS = ("x", "y", "chan")
NN = (((1,), (0,)), ((), ()))
NT = (((1,), (1,)), ((), ()))
TN = (((0,), (0,)), ((), ()))
VMEM = pl.BlockSpec(memory_space=pltpu.VMEM)
SMEM = pl.BlockSpec(memory_space=pltpu.SMEM)
HBM = pl.BlockSpec(memory_space=pltpu.HBM)


def params(mebibytes):
    return pltpu.CompilerParams(vmem_limit_bytes=mebibytes << 20)


def mul(left, right, dims, precision=None):
    return lax.dot_general(
        left, right, dims, precision=precision, preferred_element_type=F32
    )


def upper_tiles():
    for top in range(0, ORDER, BLOCK):
        for row in range(top, top + BLOCK, 8):
            for col in range(top, ORDER, 128):
                yield row, col


def split(value):
    high = value.astype(BF16)
    return high, (value - high.astype(F32)).astype(BF16)


def gram_kernel(size, start, place_ref, p0_ref, p1_ref, p2_ref, p3_ref, *refs):
    group = CH // 4
    pieces = (p0_ref, p1_ref, p2_ref, p3_ref)
    strips = [
        pl.ds(pl.multiple_of((place_ref[0] + 4 - away) % 4 * group, group), group) for away in range(4)
    ]
    bulk = []
    if start is None:
        x_ref, g, cross, h0, l0, h1, l1 = refs
        base = 0
        g[...] = jnp.zeros_like(g)
        cross[...] = jnp.zeros_like(cross)
        for strip, piece in zip(strips, pieces):
            x_ref[strip, :] = piece[...]
    else:
        before_ref, sofar_ref, mixed_ref, *refs = refs
        x_ref, keep_ref, send_ref, h0, l0, h1, l1, g, cross, sems = refs
        base = start
        early = []
        for part, first, count, into in ((0, 0, EARLY, early), (1, EARLY, size + PAD - EARLY, bulk)):
            for away, (strip, piece) in enumerate(zip(strips, pieces)):
                to = x_ref.at[strip, pl.ds(base + first, count)]
                into.append(
                    pltpu.make_async_copy(piece.at[:, pl.ds(first, count)], to, sems.at[part, away])
                )
        for copy in early + bulk:
            copy.start()
        g[...] = sofar_ref[...]
        cross[...] = mixed_ref[...]
        x_ref[:, :start] = before_ref[:, :start]
        for copy in early:
            copy.wait()

    def prepare(at, high_ref, low_ref):
        window = x_ref[:, pl.ds(at, STEP + PAD)]
        first = window[:, :STEP]
        root = lax.rsqrt(1.0 + jnp.sum(first * first, 0, keepdims=True) * (1.0 / CH))
        for k in range(BR):
            high, low = split(window[:, k : k + STEP] * root)
            high_ref[k * CH : (k + 1) * CH, :] = high
            low_ref[k * CH : (k + 1) * CH, :] = low

    def accumulate(high_ref, low_ref):
        for index, top in enumerate(range(0, ORDER, BLOCK)):
            end = top + BLOCK
            rows, cols = slice(top, end), slice(top, ORDER)
            both = mul(high_ref[rows, :], high_ref[cols, :], NT)
            mixed = mul(high_ref[rows, :], low_ref[cols, :], NT)
            g[rows, rows] += both[:, :BLOCK]
            cross[index] += mixed[:, :BLOCK]
            if end < ORDER:
                rest = slice(end, ORDER)
                other = mul(low_ref[rows, :], high_ref[rest, :], NT)
                g[rows, rest] += both[:, BLOCK:] + mixed[:, BLOCK:] + other

    prepare(base, h0, l0)

    def pair(j, carry):
        at = base + j * (2 * STEP)
        if bulk:

            @pl.when(j == 1)
            def _():
                for copy in bulk:
                    copy.wait()

        prepare(pl.multiple_of(at + STEP, STEP), h1, l1)
        accumulate(h0, l0)
        after = jnp.minimum(at + 2 * STEP, base + size - STEP)
        prepare(pl.multiple_of(after, STEP), h0, l0)
        accumulate(h1, l1)
        return carry

    lax.fori_loop(0, size // (2 * STEP), pair, 0)
    if start is None:
        return
    for index, top in enumerate(range(0, ORDER, BLOCK)):
        rows = slice(top, top + BLOCK)
        g[rows, rows] += cross[index] + cross[index].T
    scale = 1.0 / ((base + size) * 128)
    for core in range(2):

        @pl.when(place_ref[1] == core)
        def _():
            for tile, (row, col) in enumerate(upper_tiles()):
                half, piece, at = where(tile)
                to_ref = keep_ref if half == core else send_ref
                to_ref[piece, at : at + 8, :] = g[row : row + 8, col : col + 128] * scale


def where(tile):
    piece, at = divmod(tile, TILES // 128)
    return piece // 64, piece % 64, 8 * at


def gram_chunk(place, pieces, before=None):
    size = pieces[1].shape[1] - PAD
    slab = pltpu.VMEM((ORDER, STEP), BF16)
    square, blocks = (ORDER, ORDER), (ORDER // BLOCK, BLOCK, BLOCK)
    gram, mixed = jax.ShapeDtypeStruct(square, F32), jax.ShapeDtypeStruct(blocks, F32)
    half = jax.ShapeDtypeStruct((64, 8 * TILES // 128, 128), F32)
    if before is None:
        start, given, into, out, scratch = None, [], VMEM, (gram, mixed), []
    else:
        start, given, into, out = before[0].shape[1] - PAD, list(before), HBM, (half, half)
        pieces = [pltpu.with_memory_space_constraint(piece, pltpu.HBM) for piece in pieces]
        scratch = [pltpu.VMEM(square, F32), pltpu.VMEM(blocks, F32), pltpu.SemaphoreType.DMA((2, 4))]
    x = jax.ShapeDtypeStruct((CH, size + PAD + (start or 0)), F32)
    return pl.pallas_call(
        functools.partial(gram_kernel, size, start),
        out_shape=(x,) + out,
        in_specs=[SMEM] + [into] * 4 + [VMEM] * len(given),
        out_specs=(VMEM,) * 3,
        scratch_shapes=[slab] * 4 + scratch,
        compiler_params=params(32),
        name="gram_first" if start is None else "gram_last",
    )(place, *pieces, *given)


def lane(value, j):
    return jnp.broadcast_to(value[:, j : j + 1], (8, 128))


def row(value, j):
    return jnp.broadcast_to(value[j : j + 1, :], (8, 128))


def diagonal_factor(d):
    n = PANEL // 8
    rows = lax.broadcasted_iota(jnp.int32, (8, 128), 0)
    cols = lax.broadcasted_iota(jnp.int32, (8, 128), 1)
    w = [jnp.where(cols == rows + 8 * i, 1.0, 0.0).astype(F32) for i in range(n)]
    upper, inverse = [], []
    for g in range(n):
        cg = [lane(d[g], 8 * g + j) for j in range(8)]
        below = range(g + 1, n)
        cb = {i: [lane(d[i], 8 * g + j) for j in range(8)] for i in below}
        dg, wg = d[g], w[g]
        tops, inv = [], []
        pivots = jnp.zeros((8, 128), F32)
        for j in range(8):
            pivot = row(cg[j], j)
            r = 1.0 / pivot
            inv.append(r)
            pivots = jnp.where(rows == j, pivot, pivots)
            m = jnp.where(rows > j, cg[j] * r, 0.0)
            top = {k: row(cg[k], j) for k in range(j + 1, 8)}
            tops.append(top)
            for k in range(j + 1, 8):
                cg[k] = cg[k] - m * top[k]
            dg = dg - m * row(dg, j)
            wg = wg - m * row(wg, j)
        scale = lax.rsqrt(pivots)
        upper.append(jnp.where(cols >= rows + 8 * g, dg * scale, 0.0))
        inverse.append(wg * scale)
        ds = [row(dg, j) for j in range(8)]
        ws = [row(wg, j) for j in range(8)]
        for i in below:
            c, di, wi = cb[i], d[i], w[i]
            for j in range(8):
                m = c[j] * inv[j]
                for k in range(j + 1, 8):
                    c[k] = c[k] - m * tops[j][k]
                di = di - m * ds[j]
                wi = wi - m * ws[j]
            d[i], w[i] = di, wi
    return upper, inverse


def factor_kernel(
    place_ref, own_ref, other_ref, given_ref, mine_ref, basis_ref, a, u, inverse_ref, start_ref, sem
):
    p = pl.program_id(0)
    last = ORDER // PANEL - 1
    fetch = pltpu.make_async_copy(given_ref, start_ref, sem.at[0])

    @pl.when(p == 0)
    def _():
        fetch.start()
        for core in range(2):

            @pl.when(place_ref[1] == core)
            def _():
                for tile, (r, c) in enumerate(upper_tiles()):
                    half, piece, at = where(tile)
                    from_ref = own_ref if half == core else other_ref
                    a[r : r + 8, c : c + 128] = from_ref[piece, at : at + 8, :]

    o = pl.multiple_of(p * PANEL, PANEL)
    strips = [pl.ds(pl.multiple_of(o + 8 * i, 8), 8) for i in range(PANEL // 8)]
    upper, inverse = diagonal_factor([a[s, pl.ds(o, PANEL)] for s in strips])
    for i, s in enumerate(strips):
        u[s, pl.ds(o, PANEL)] = upper[i]
        inverse_ref[8 * i : 8 * i + 8, :] = inverse[i]
    for q in range(ORDER // PANEL - 1):

        @pl.when(p == q)
        def _():
            top, s = q * PANEL, (q + 1) * PANEL
            panel = mul(inverse_ref[...], a[top:s, s:], NN, EXACT)
            u[top:s, s:] = panel
            high, low = split(panel)
            for b in range(s, ORDER, BLOCK):
                rows, cols = slice(b - s, min(b + BLOCK, ORDER) - s), slice(b - s, ORDER - s)
                term = mul(high[:, rows], high[:, cols], TN)
                term += mul(high[:, rows], low[:, cols], TN)
                a[b : b + BLOCK, b:] -= term + mul(low[:, rows], high[:, cols], TN)

    @pl.when(p == last)
    def _():
        share = mine_ref.shape[0]
        top = pl.multiple_of(place_ref[0] * share, share)
        below = lax.broadcasted_iota(jnp.int32, mine_ref.shape, 0) + top
        cols = lax.broadcasted_iota(jnp.int32, mine_ref.shape, 1)
        mine_ref[...] = jnp.where(cols >= below, u[pl.ds(top, share), :], 0.0)
        for q in range(HALF // PANEL, last):
            s = (q + 1) * PANEL
            u[s:, q * PANEL : s] = jnp.zeros((ORDER - s, PANEL), F32)
        fetch.wait()
        lead = mul(start_ref[...], u[HALF:, HALF:], TN, EXACT)
        basis = lead / jnp.sqrt(jnp.sum(lead * lead))
        inner = mul(basis, basis, NT, EXACT)
        states = inner.shape[0]
        eye = jnp.where(
            lax.broadcasted_iota(jnp.int32, (states, states), 0)
            == lax.broadcasted_iota(jnp.int32, (states, states), 1),
            1.5,
            0.0,
        ).astype(F32)
        total = None
        for step in range(NSTEPS):
            m = eye - 0.5 * inner
            total = m if total is None else mul(total, m, NN, EXACT)
            if step < NSTEPS - 1:
                inner = mul(mul(inner, m, NN, EXACT), m, NN, EXACT)
        basis_ref[...] = mul(total, basis, NN, EXACT)


def factor_and_basis(place, own, other, start, share):
    whole = lambda shape: pl.BlockSpec(shape, lambda i: (0,) * len(shape))
    states = start.shape[1]
    return pl.pallas_call(
        factor_kernel,
        grid=(ORDER // PANEL,),
        out_shape=(
            jax.ShapeDtypeStruct((share, ORDER), F32),
            jax.ShapeDtypeStruct((states, HALF), F32),
        ),
        in_specs=[SMEM, whole(own.shape), whole(other.shape), HBM],
        out_specs=(whole((share, ORDER)), whole((states, HALF))),
        scratch_shapes=[
            pltpu.VMEM((ORDER, ORDER), F32),
            pltpu.VMEM((ORDER, ORDER), F32),
            pltpu.VMEM((PANEL, PANEL), F32),
            pltpu.VMEM(start.shape, F32),
            pltpu.SemaphoreType.DMA((1,)),
        ],
        compiler_params=params(32),
        name="factor",
    )(place, own, other, pltpu.with_memory_space_constraint(start, pltpu.HBM))


def states_kernel(basis_ref, x_ref, out_ref, high_ref, low_ref):
    span = out_ref.shape[1]
    start = pl.multiple_of(pl.program_id(0) * span, span)
    window = x_ref[:, pl.ds(start, span + PAD)]
    first = BR // 2
    for k in range(first):
        high, low = split(window[:, first + k : first + k + span])
        high_ref[k * CH : (k + 1) * CH, :] = high
        low_ref[k * CH : (k + 1) * CH, :] = low
    bh, bl = split(basis_ref[...])
    out = mul(bh, high_ref[...], NN)
    out += mul(bl, high_ref[...], NN)
    out_ref[...] = out + mul(bh, low_ref[...], NN)


def project(basis, x):
    states = basis.shape[0]
    count = x.shape[1] - PAD
    span = 2048
    slab = pltpu.VMEM((HALF, span), BF16)
    return pl.pallas_call(
        states_kernel,
        grid=(count // span,),
        out_shape=jax.ShapeDtypeStruct((states, count), F32),
        in_specs=[
            pl.BlockSpec(basis.shape, lambda i: (0, 0)),
            pl.BlockSpec(x.shape, lambda i: (0, 0)),
        ],
        out_specs=pl.BlockSpec((states, span), lambda i: (0, i)),
        scratch_shapes=[slab, slab],
        compiler_params=params(32),
        name="states",
    )(basis, x)


def windows(samples, halo, first, width, nearest):
    chans, chan = lax.axis_size("chan"), lax.axis_index("chan")
    count = samples.shape[1] // chans
    owed = []
    for away in range(nearest, chans):
        to = (chan + away) % chans
        window = lax.dynamic_slice_in_dim(samples, to * count + first, width, 1)
        if halo is not None:
            end = jnp.minimum((to + 1) * count, samples.shape[1] - PAD)
            tail = lax.dynamic_slice_in_dim(samples, end, PAD, 1)
            window = jnp.concatenate([window, jnp.where(to == chans - 1, halo, tail)], 1)
        owed.append(window)
    return owed


def exchange(owed):
    chans = lax.axis_size("chan")
    return [
        lax.ppermute(window, "chan", [(i, (i + away) % chans) for i in range(chans)])
        for away, window in enumerate(owed, 1)
    ]


def per_device(samples, start_basis):
    times, chans = lax.axis_size(TIME), lax.axis_size("chan")
    count = samples.shape[1] // chans
    core = lax.axis_index("core")
    place = jnp.stack([lax.axis_index("chan"), core]).astype(jnp.int32)
    halo = lax.ppermute(samples[:, :PAD], TIME, [(i, i - 1) for i in range(1, times)])
    own, *owed = windows(samples, None, 0, CHUNK + PAD, 0)
    pieces = [own] + exchange(owed)
    own, *owed = windows(samples, halo, CHUNK, count - CHUNK, 0)
    others = [own] + exchange(owed)
    before = gram_chunk(place, pieces)
    x, keep, send = gram_chunk(place, others, before)
    swap = [(0, 1), (1, 0)]
    half = keep + lax.ppermute(send, "core", swap)
    half = lax.all_to_all(half, CHIPS, 0, 0, tiled=True)
    half = jnp.broadcast_to(jnp.sum(half, 0)[None], half.shape)
    half = lax.all_to_all(half, CHIPS, 0, 0, tiled=True)
    other = lax.ppermute(half, "core", swap)
    place = jnp.stack([lax.axis_index(ALL), core]).astype(jnp.int32)
    mine, basis = factor_and_basis(place, half, other, start_basis, ORDER // (times * chans))
    return (mine, project(basis, x))


def solution(mesh):
    mesh = Mesh(mesh.devices.reshape(4, 4, 2, 4), ALL)
    return jax.shard_map(
        per_device,
        mesh=mesh,
        in_specs=(P("chan", TIME), P()),
        out_specs=(P(ALL, None), P(None, ALL)),
        check_vma=False,
    )
```

```python
import functools

import jax
import jax.numpy as jnp
from jax import lax
from jax.experimental import pallas as pl
from jax.experimental.pallas import tpu as pltpu
from jax.sharding import Mesh
from jax.sharding import PartitionSpec as P

BR = 16
NSTEPS = 6
CH = 64
ORDER = 1024
HALF = 512
PANEL = 128
BLOCK = 256
PAD = 128
STEP = 512
CHUNK = 3072
EARLY = 1664
TILES = 640
F32 = jnp.float32
BF16 = jnp.bfloat16
EXACT = lax.Precision.HIGHEST
ALL = ("x", "y", "core", "chan")
TIME = ("x", "y", "core")
CHIPS = ("x", "y", "chan")
NN = (((1,), (0,)), ((), ()))
NT = (((1,), (1,)), ((), ()))
TN = (((0,), (0,)), ((), ()))
VMEM = pl.BlockSpec(memory_space=pltpu.VMEM)
SMEM = pl.BlockSpec(memory_space=pltpu.SMEM)
HBM = pl.BlockSpec(memory_space=pltpu.HBM)


def params(mebibytes):
    return pltpu.CompilerParams(vmem_limit_bytes=mebibytes << 20)


def mul(left, right, dims, precision=None):
    return lax.dot_general(
        left, right, dims, precision=precision, preferred_element_type=F32
    )


def upper_tiles():
    for top in range(0, ORDER, BLOCK):
        for row in range(top, top + BLOCK, 8):
            for col in range(top, ORDER, 128):
                yield row, col


def split(value):
    high = value.astype(BF16)
    return high, (value - high.astype(F32)).astype(BF16)


def gram_kernel(size, start, place_ref, p0_ref, p1_ref, p2_ref, p3_ref, *refs):
    group = CH // 4
    pieces = (p0_ref, p1_ref, p2_ref, p3_ref)
    strips = [
        pl.ds(pl.multiple_of((place_ref[0] + 4 - away) % 4 * group, group), group) for away in range(4)
    ]
    bulk = []
    if start is None:
        x_ref, g, cross, h0, l0, h1, l1 = refs
        base = 0
        g[...] = jnp.zeros_like(g)
        cross[...] = jnp.zeros_like(cross)
        for strip, piece in zip(strips, pieces):
            x_ref[strip, :] = piece[...]
    else:
        before_ref, sofar_ref, mixed_ref, *refs = refs
        x_ref, keep_ref, send_ref, h0, l0, h1, l1, g, cross, sems = refs
        base = start
        early = []
        for part, first, count, into in ((0, 0, EARLY, early), (1, EARLY, size + PAD - EARLY, bulk)):
            for away, (strip, piece) in enumerate(zip(strips, pieces)):
                to = x_ref.at[strip, pl.ds(base + first, count)]
                into.append(
                    pltpu.make_async_copy(piece.at[:, pl.ds(first, count)], to, sems.at[part, away])
                )
        for copy in early + bulk:
            copy.start()
        g[...] = sofar_ref[...]
        cross[...] = mixed_ref[...]
        x_ref[:, :start] = before_ref[:, :start]
        for copy in early:
            copy.wait()

    def prepare(at, high_ref, low_ref):
        window = x_ref[:, pl.ds(at, STEP + PAD)]
        first = window[:, :STEP]
        root = lax.rsqrt(1.0 + jnp.sum(first * first, 0, keepdims=True) * (1.0 / CH))
        for k in range(BR):
            high, low = split(window[:, k : k + STEP] * root)
            high_ref[k * CH : (k + 1) * CH, :] = high
            low_ref[k * CH : (k + 1) * CH, :] = low

    def accumulate(high_ref, low_ref):
        for index, top in enumerate(range(0, ORDER, BLOCK)):
            end = top + BLOCK
            rows, cols = slice(top, end), slice(top, ORDER)
            both = mul(high_ref[rows, :], high_ref[cols, :], NT)
            mixed = mul(high_ref[rows, :], low_ref[cols, :], NT)
            g[rows, rows] += both[:, :BLOCK]
            cross[index] += mixed[:, :BLOCK]
            if end < ORDER:
                rest = slice(end, ORDER)
                other = mul(low_ref[rows, :], high_ref[rest, :], NT)
                g[rows, rest] += both[:, BLOCK:] + mixed[:, BLOCK:] + other

    prepare(base, h0, l0)

    def pair(j, carry):
        at = base + j * (2 * STEP)
        if bulk:

            @pl.when(j == 1)
            def _():
                for copy in bulk:
                    copy.wait()

        prepare(pl.multiple_of(at + STEP, STEP), h1, l1)
        accumulate(h0, l0)
        after = jnp.minimum(at + 2 * STEP, base + size - STEP)
        prepare(pl.multiple_of(after, STEP), h0, l0)
        accumulate(h1, l1)
        return carry

    lax.fori_loop(0, size // (2 * STEP), pair, 0)
    if start is None:
        return
    for index, top in enumerate(range(0, ORDER, BLOCK)):
        rows = slice(top, top + BLOCK)
        g[rows, rows] += cross[index] + cross[index].T
    scale = 1.0 / ((base + size) * 128)
    for core in range(2):

        @pl.when(place_ref[1] == core)
        def _():
            for tile, (row, col) in enumerate(upper_tiles()):
                half, piece, at = where(tile)
                to_ref = keep_ref if half == core else send_ref
                to_ref[piece, at : at + 8, :] = g[row : row + 8, col : col + 128] * scale


def where(tile):
    piece, at = divmod(tile, TILES // 128)
    return piece // 64, piece % 64, 8 * at


def gram_chunk(place, pieces, before=None):
    size = pieces[1].shape[1] - PAD
    slab = pltpu.VMEM((ORDER, STEP), BF16)
    square, blocks = (ORDER, ORDER), (ORDER // BLOCK, BLOCK, BLOCK)
    gram, mixed = jax.ShapeDtypeStruct(square, F32), jax.ShapeDtypeStruct(blocks, F32)
    half = jax.ShapeDtypeStruct((64, 8 * TILES // 128, 128), F32)
    if before is None:
        start, given, into, out, scratch = None, [], VMEM, (gram, mixed), []
    else:
        start, given, into, out = before[0].shape[1] - PAD, list(before), HBM, (half, half)
        pieces = [pltpu.with_memory_space_constraint(piece, pltpu.HBM) for piece in pieces]
        scratch = [pltpu.VMEM(square, F32), pltpu.VMEM(blocks, F32), pltpu.SemaphoreType.DMA((2, 4))]
    x = jax.ShapeDtypeStruct((CH, size + PAD + (start or 0)), F32)
    return pl.pallas_call(
        functools.partial(gram_kernel, size, start),
        out_shape=(x,) + out,
        in_specs=[SMEM] + [into] * 4 + [VMEM] * len(given),
        out_specs=(VMEM,) * 3,
        scratch_shapes=[slab] * 4 + scratch,
        compiler_params=params(32),
        name="gram_first" if start is None else "gram_last",
    )(place, *pieces, *given)


def lane(value, j):
    return jnp.broadcast_to(value[:, j : j + 1], (8, 128))


def row(value, j):
    return jnp.broadcast_to(value[j : j + 1, :], (8, 128))


def diagonal_factor(d):
    n = PANEL // 8
    rows = lax.broadcasted_iota(jnp.int32, (8, 128), 0)
    cols = lax.broadcasted_iota(jnp.int32, (8, 128), 1)
    w = [jnp.where(cols == rows + 8 * i, 1.0, 0.0).astype(F32) for i in range(n)]
    upper, inverse = [], []
    cn = [lane(d[0], j) for j in range(8)]
    for g in range(n):
        cg = cn
        below = range(g + 1, n)
        cb = {i: [lane(d[i], 8 * g + j) for j in range(8)] for i in below}
        if g + 1 < n:
            cn = [lane(d[g + 1], 8 * (g + 1) + k) for k in range(8)]
        dg, wg = d[g], w[g]
        tops, inv = [], []
        pivots = jnp.zeros((8, 128), F32)
        for j in range(8):
            pivot = row(cg[j], j)
            r = 1.0 / pivot
            inv.append(r)
            pivots = jnp.where(rows == j, pivot, pivots)
            under = jnp.where(rows > j, cg[j], 0.0)
            top = {k: row(cg[k], j) for k in range(j + 1, 8)}
            tops.append(top)
            for k in range(j + 1, 8):
                cg[k] = cg[k] - (under * top[k]) * r
            dg = dg - (under * row(dg, j)) * r
            wg = wg - (under * row(wg, j)) * r
        scale = lax.rsqrt(pivots)
        upper.append(jnp.where(cols >= rows + 8 * g, dg * scale, 0.0))
        inverse.append(wg * scale)
        ds = [row(dg, j) for j in range(8)]
        ws = [row(wg, j) for j in range(8)]
        for i in below:
            c, di, wi = cb[i], d[i], w[i]
            for j in range(8):
                m = c[j] * inv[j]
                if i == g + 1:
                    cn = [cn[k] - m * row(c[j], k) for k in range(8)]
                for k in range(j + 1, 8):
                    c[k] = c[k] - m * tops[j][k]
                di = di - m * ds[j]
                wi = wi - m * ws[j]
            d[i], w[i] = di, wi
    return upper, inverse


def factor_kernel(
    place_ref, own_ref, other_ref, given_ref, mine_ref, basis_ref, a, u, inverse_ref, start_ref, sem
):
    p = pl.program_id(0)
    last = ORDER // PANEL - 1
    fetch = pltpu.make_async_copy(given_ref, start_ref, sem.at[0])

    @pl.when(p == 0)
    def _():
        fetch.start()
        for core in range(2):

            @pl.when(place_ref[1] == core)
            def _():
                for tile, (r, c) in enumerate(upper_tiles()):
                    half, piece, at = where(tile)
                    from_ref = own_ref if half == core else other_ref
                    a[r : r + 8, c : c + 128] = from_ref[piece, at : at + 8, :]

    o = pl.multiple_of(p * PANEL, PANEL)
    strips = [pl.ds(pl.multiple_of(o + 8 * i, 8), 8) for i in range(PANEL // 8)]
    upper, inverse = diagonal_factor([a[s, pl.ds(o, PANEL)] for s in strips])
    for i, s in enumerate(strips):
        u[s, pl.ds(o, PANEL)] = upper[i]
        inverse_ref[8 * i : 8 * i + 8, :] = inverse[i]
    for q in range(ORDER // PANEL - 1):

        @pl.when(p == q)
        def _():
            top, s = q * PANEL, (q + 1) * PANEL
            panel = mul(inverse_ref[...], a[top:s, s:], NN, EXACT)
            u[top:s, s:] = panel
            high, low = split(panel)
            for b in range(s, ORDER, BLOCK):
                rows, cols = slice(b - s, min(b + BLOCK, ORDER) - s), slice(b - s, ORDER - s)
                term = mul(high[:, rows], high[:, cols], TN)
                term += mul(high[:, rows], low[:, cols], TN)
                a[b : b + BLOCK, b:] -= term + mul(low[:, rows], high[:, cols], TN)

    @pl.when(p == last)
    def _():
        share = mine_ref.shape[0]
        top = pl.multiple_of(place_ref[0] * share, share)
        below = lax.broadcasted_iota(jnp.int32, mine_ref.shape, 0) + top
        cols = lax.broadcasted_iota(jnp.int32, mine_ref.shape, 1)
        mine_ref[...] = jnp.where(cols >= below, u[pl.ds(top, share), :], 0.0)
        for q in range(HALF // PANEL, last):
            s = (q + 1) * PANEL
            u[s:, q * PANEL : s] = jnp.zeros((ORDER - s, PANEL), F32)
        fetch.wait()
        lead = mul(start_ref[...], u[HALF:, HALF:], TN, EXACT)
        basis = lead / jnp.sqrt(jnp.sum(lead * lead))
        inner = mul(basis, basis, NT, EXACT)
        states = inner.shape[0]
        eye = jnp.where(
            lax.broadcasted_iota(jnp.int32, (states, states), 0)
            == lax.broadcasted_iota(jnp.int32, (states, states), 1),
            1.5,
            0.0,
        ).astype(F32)
        total = None
        for step in range(NSTEPS):
            m = eye - 0.5 * inner
            total = m if total is None else mul(total, m, NN, EXACT)
            if step < NSTEPS - 1:
                inner = mul(mul(inner, m, NN, EXACT), m, NN, EXACT)
        basis_ref[...] = mul(total, basis, NN, EXACT)


def factor_and_basis(place, own, other, start, share):
    whole = lambda shape: pl.BlockSpec(shape, lambda i: (0,) * len(shape))
    states = start.shape[1]
    return pl.pallas_call(
        factor_kernel,
        grid=(ORDER // PANEL,),
        out_shape=(
            jax.ShapeDtypeStruct((share, ORDER), F32),
            jax.ShapeDtypeStruct((states, HALF), F32),
        ),
        in_specs=[SMEM, whole(own.shape), whole(other.shape), HBM],
        out_specs=(whole((share, ORDER)), whole((states, HALF))),
        scratch_shapes=[
            pltpu.VMEM((ORDER, ORDER), F32),
            pltpu.VMEM((ORDER, ORDER), F32),
            pltpu.VMEM((PANEL, PANEL), F32),
            pltpu.VMEM(start.shape, F32),
            pltpu.SemaphoreType.DMA((1,)),
        ],
        compiler_params=params(32),
        name="factor",
    )(place, own, other, pltpu.with_memory_space_constraint(start, pltpu.HBM))


def states_kernel(basis_ref, x_ref, out_ref, high_ref, low_ref):
    span = out_ref.shape[1]
    start = pl.multiple_of(pl.program_id(0) * span, span)
    window = x_ref[:, pl.ds(start, span + PAD)]
    first = BR // 2
    for k in range(first):
        high, low = split(window[:, first + k : first + k + span])
        high_ref[k * CH : (k + 1) * CH, :] = high
        low_ref[k * CH : (k + 1) * CH, :] = low
    bh, bl = split(basis_ref[...])
    out = mul(bh, high_ref[...], NN)
    out += mul(bl, high_ref[...], NN)
    out_ref[...] = out + mul(bh, low_ref[...], NN)


def project(basis, x):
    states = basis.shape[0]
    count = x.shape[1] - PAD
    span = 2048
    slab = pltpu.VMEM((HALF, span), BF16)
    return pl.pallas_call(
        states_kernel,
        grid=(count // span,),
        out_shape=jax.ShapeDtypeStruct((states, count), F32),
        in_specs=[
            pl.BlockSpec(basis.shape, lambda i: (0, 0)),
            pl.BlockSpec(x.shape, lambda i: (0, 0)),
        ],
        out_specs=pl.BlockSpec((states, span), lambda i: (0, i)),
        scratch_shapes=[slab, slab],
        compiler_params=params(32),
        name="states",
    )(basis, x)


def windows(samples, halo, first, width, nearest):
    chans, chan = lax.axis_size("chan"), lax.axis_index("chan")
    count = samples.shape[1] // chans
    owed = []
    for away in range(nearest, chans):
        to = (chan + away) % chans
        window = lax.dynamic_slice_in_dim(samples, to * count + first, width, 1)
        if halo is not None:
            end = jnp.minimum((to + 1) * count, samples.shape[1] - PAD)
            tail = lax.dynamic_slice_in_dim(samples, end, PAD, 1)
            window = jnp.concatenate([window, jnp.where(to == chans - 1, halo, tail)], 1)
        owed.append(window)
    return owed


def exchange(owed):
    chans = lax.axis_size("chan")
    return [
        lax.ppermute(window, "chan", [(i, (i + away) % chans) for i in range(chans)])
        for away, window in enumerate(owed, 1)
    ]


def per_device(samples, start_basis):
    times, chans = lax.axis_size(TIME), lax.axis_size("chan")
    count = samples.shape[1] // chans
    core = lax.axis_index("core")
    place = jnp.stack([lax.axis_index("chan"), core]).astype(jnp.int32)
    halo = lax.ppermute(samples[:, :PAD], TIME, [(i, i - 1) for i in range(1, times)])
    own, *owed = windows(samples, None, 0, CHUNK + PAD, 0)
    pieces = [own] + exchange(owed)
    own, *owed = windows(samples, halo, CHUNK, count - CHUNK, 0)
    others = [own] + exchange(owed)
    before = gram_chunk(place, pieces)
    x, keep, send = gram_chunk(place, others, before)
    swap = [(0, 1), (1, 0)]
    half = keep + lax.ppermute(send, "core", swap)
    half = lax.all_to_all(half, CHIPS, 0, 0, tiled=True)
    half = jnp.broadcast_to(jnp.sum(half, 0)[None], half.shape)
    half = lax.all_to_all(half, CHIPS, 0, 0, tiled=True)
    other = lax.ppermute(half, "core", swap)
    place = jnp.stack([lax.axis_index(ALL), core]).astype(jnp.int32)
    mine, basis = factor_and_basis(place, half, other, start_basis, ORDER // (times * chans))
    return (mine, project(basis, x))


def solution(mesh):
    mesh = Mesh(mesh.devices.reshape(4, 4, 2, 4), ALL)
    return jax.shard_map(
        per_device,
        mesh=mesh,
        in_specs=(P("chan", TIME), P()),
        out_specs=(P(ALL, None), P(None, ALL)),
        check_vma=False,
    )
```

```python
import functools

import jax
import jax.numpy as jnp
from jax import lax
from jax.experimental import pallas as pl
from jax.experimental.pallas import tpu as pltpu
from jax.sharding import Mesh
from jax.sharding import PartitionSpec as P

BR = 16
NSTEPS = 6
CH = 64
ORDER = 1024
HALF = 512
PANEL = 128
BLOCK = 256
PAD = 128
STEP = 512
CHUNK = 2048
EARLY = 1664
TILES = 640
F32 = jnp.float32
BF16 = jnp.bfloat16
EXACT = lax.Precision.HIGHEST
ALL = ("x", "y", "core", "chan")
TIME = ("x", "y", "core")
CHIPS = ("x", "y", "chan")
NN = (((1,), (0,)), ((), ()))
NT = (((1,), (1,)), ((), ()))
TN = (((0,), (0,)), ((), ()))
VMEM = pl.BlockSpec(memory_space=pltpu.VMEM)
SMEM = pl.BlockSpec(memory_space=pltpu.SMEM)
HBM = pl.BlockSpec(memory_space=pltpu.HBM)


def params(mebibytes):
    return pltpu.CompilerParams(vmem_limit_bytes=mebibytes << 20)


def mul(left, right, dims, precision=None):
    return lax.dot_general(
        left, right, dims, precision=precision, preferred_element_type=F32
    )


def upper_tiles():
    for top in range(0, ORDER, BLOCK):
        for row in range(top, top + BLOCK, 8):
            for col in range(top, ORDER, 128):
                yield row, col


def split(value):
    high = value.astype(BF16)
    return high, (value - high.astype(F32)).astype(BF16)


def gram_kernel(size, start, place_ref, p0_ref, p1_ref, p2_ref, p3_ref, *refs):
    group = CH // 4
    pieces = (p0_ref, p1_ref, p2_ref, p3_ref)
    strips = [
        pl.ds(pl.multiple_of((place_ref[0] + 4 - away) % 4 * group, group), group) for away in range(4)
    ]
    bulk = []
    if start is None:
        x_ref, g, cross, h0, l0, h1, l1 = refs
        base = 0
        g[...] = jnp.zeros_like(g)
        cross[...] = jnp.zeros_like(cross)
        for strip, piece in zip(strips, pieces):
            x_ref[strip, :] = piece[...]
    else:
        before_ref, sofar_ref, mixed_ref, *refs = refs
        x_ref, keep_ref, send_ref, h0, l0, h1, l1, g, cross, sems = refs
        base = start
        early = []
        for part, first, count, into in ((0, 0, EARLY, early), (1, EARLY, size + PAD - EARLY, bulk)):
            for away, (strip, piece) in enumerate(zip(strips, pieces)):
                to = x_ref.at[strip, pl.ds(base + first, count)]
                into.append(
                    pltpu.make_async_copy(piece.at[:, pl.ds(first, count)], to, sems.at[part, away])
                )
        for copy in early + bulk:
            copy.start()
        g[...] = sofar_ref[...]
        cross[...] = mixed_ref[...]
        x_ref[:, :start] = before_ref[:, :start]
        for copy in early:
            copy.wait()

    def prepare(at, high_ref, low_ref):
        window = x_ref[:, pl.ds(at, STEP + PAD)]
        first = window[:, :STEP]
        root = lax.rsqrt(1.0 + jnp.sum(first * first, 0, keepdims=True) * (1.0 / CH))
        for k in range(BR):
            high, low = split(window[:, k : k + STEP] * root)
            high_ref[k * CH : (k + 1) * CH, :] = high
            low_ref[k * CH : (k + 1) * CH, :] = low

    def accumulate(high_ref, low_ref):
        for index, top in enumerate(range(0, ORDER, BLOCK)):
            end = top + BLOCK
            rows, cols = slice(top, end), slice(top, ORDER)
            both = mul(high_ref[rows, :], high_ref[cols, :], NT)
            mixed = mul(high_ref[rows, :], low_ref[cols, :], NT)
            g[rows, rows] += both[:, :BLOCK]
            cross[index] += mixed[:, :BLOCK]
            if end < ORDER:
                rest = slice(end, ORDER)
                other = mul(low_ref[rows, :], high_ref[rest, :], NT)
                g[rows, rest] += both[:, BLOCK:] + mixed[:, BLOCK:] + other

    prepare(base, h0, l0)

    def pair(j, carry):
        at = base + j * (2 * STEP)
        if bulk:

            @pl.when(j == 1)
            def _():
                for copy in bulk:
                    copy.wait()

        prepare(pl.multiple_of(at + STEP, STEP), h1, l1)
        accumulate(h0, l0)
        after = jnp.minimum(at + 2 * STEP, base + size - STEP)
        prepare(pl.multiple_of(after, STEP), h0, l0)
        accumulate(h1, l1)
        return carry

    lax.fori_loop(0, size // (2 * STEP), pair, 0)
    if start is None:
        return
    for index, top in enumerate(range(0, ORDER, BLOCK)):
        rows = slice(top, top + BLOCK)
        g[rows, rows] += cross[index] + cross[index].T
    scale = 1.0 / ((base + size) * 128)
    for core in range(2):

        @pl.when(place_ref[1] == core)
        def _():
            for tile, (row, col) in enumerate(upper_tiles()):
                half, piece, at = where(tile)
                to_ref = keep_ref if half == core else send_ref
                to_ref[piece, at : at + 8, :] = g[row : row + 8, col : col + 128] * scale


def where(tile):
    piece, at = divmod(tile, TILES // 128)
    return piece // 64, piece % 64, 8 * at


def gram_chunk(place, pieces, before=None):
    size = pieces[1].shape[1] - PAD
    slab = pltpu.VMEM((ORDER, STEP), BF16)
    square, blocks = (ORDER, ORDER), (ORDER // BLOCK, BLOCK, BLOCK)
    gram, mixed = jax.ShapeDtypeStruct(square, F32), jax.ShapeDtypeStruct(blocks, F32)
    half = jax.ShapeDtypeStruct((64, 8 * TILES // 128, 128), F32)
    if before is None:
        start, given, into, out, scratch = None, [], VMEM, (gram, mixed), []
    else:
        start, given, into, out = before[0].shape[1] - PAD, list(before), HBM, (half, half)
        pieces = [pltpu.with_memory_space_constraint(piece, pltpu.HBM) for piece in pieces]
        scratch = [pltpu.VMEM(square, F32), pltpu.VMEM(blocks, F32), pltpu.SemaphoreType.DMA((2, 4))]
    x = jax.ShapeDtypeStruct((CH, size + PAD + (start or 0)), F32)
    return pl.pallas_call(
        functools.partial(gram_kernel, size, start),
        out_shape=(x,) + out,
        in_specs=[SMEM] + [into] * 4 + [VMEM] * len(given),
        out_specs=(VMEM,) * 3,
        scratch_shapes=[slab] * 4 + scratch,
        compiler_params=params(32),
        name="gram_first" if start is None else "gram_last",
    )(place, *pieces, *given)


def lane(value, j):
    return jnp.broadcast_to(value[:, j : j + 1], (8, 128))


def row(value, j):
    return jnp.broadcast_to(value[j : j + 1, :], (8, 128))


def diagonal_factor(d):
    n = PANEL // 8
    rows = lax.broadcasted_iota(jnp.int32, (8, 128), 0)
    cols = lax.broadcasted_iota(jnp.int32, (8, 128), 1)
    w = [jnp.where(cols == rows + 8 * i, 1.0, 0.0).astype(F32) for i in range(n)]
    upper, inverse = [], []
    cn = [lane(d[0], j) for j in range(8)]
    for g in range(n):
        cg = cn
        below = range(g + 1, n)
        cb = {i: [lane(d[i], 8 * g + j) for j in range(8)] for i in below}
        if g + 1 < n:
            cn = [lane(d[g + 1], 8 * (g + 1) + k) for k in range(8)]
        dg, wg = d[g], w[g]
        tops, inv = [], []
        pivots = jnp.zeros((8, 128), F32)
        for j in range(8):
            pivot = row(cg[j], j)
            r = 1.0 / pivot
            inv.append(r)
            pivots = jnp.where(rows == j, pivot, pivots)
            under = jnp.where(rows > j, cg[j], 0.0)
            top = {k: row(cg[k], j) for k in range(j + 1, 8)}
            tops.append(top)
            for k in range(j + 1, 8):
                cg[k] = cg[k] - (under * top[k]) * r
            dg = dg - (under * row(dg, j)) * r
            wg = wg - (under * row(wg, j)) * r
        scale = lax.rsqrt(pivots)
        upper.append(jnp.where(cols >= rows + 8 * g, dg * scale, 0.0))
        inverse.append(wg * scale)
        ds = [row(dg, j) for j in range(8)]
        ws = [row(wg, j) for j in range(8)]
        for i in below:
            c, di, wi = cb[i], d[i], w[i]
            for j in range(8):
                m = c[j] * inv[j]
                if i == g + 1:
                    cn = [cn[k] - m * row(c[j], k) for k in range(8)]
                for k in range(j + 1, 8):
                    c[k] = c[k] - m * tops[j][k]
                di = di - m * ds[j]
                wi = wi - m * ws[j]
            d[i], w[i] = di, wi
    return upper, inverse


def factor_kernel(
    place_ref, own_ref, other_ref, given_ref, mine_ref, basis_ref, a, u, inverse_ref, start_ref, sem
):
    p = pl.program_id(0)
    last = ORDER // PANEL - 1
    fetch = pltpu.make_async_copy(given_ref, start_ref, sem.at[0])

    @pl.when(p == 0)
    def _():
        fetch.start()
        for core in range(2):

            @pl.when(place_ref[1] == core)
            def _():
                for tile, (r, c) in enumerate(upper_tiles()):
                    half, piece, at = where(tile)
                    from_ref = own_ref if half == core else other_ref
                    a[r : r + 8, c : c + 128] = from_ref[piece, at : at + 8, :]

    o = pl.multiple_of(p * PANEL, PANEL)
    strips = [pl.ds(pl.multiple_of(o + 8 * i, 8), 8) for i in range(PANEL // 8)]
    upper, inverse = diagonal_factor([a[s, pl.ds(o, PANEL)] for s in strips])
    for i, s in enumerate(strips):
        u[s, pl.ds(o, PANEL)] = upper[i]
        inverse_ref[8 * i : 8 * i + 8, :] = inverse[i]
    for q in range(ORDER // PANEL - 1):

        @pl.when(p == q)
        def _():
            top, s = q * PANEL, (q + 1) * PANEL
            panel = mul(inverse_ref[...], a[top:s, s:], NN, EXACT)
            u[top:s, s:] = panel
            high, low = split(panel)
            for b in range(s, ORDER, BLOCK):
                rows, cols = slice(b - s, min(b + BLOCK, ORDER) - s), slice(b - s, ORDER - s)
                term = mul(high[:, rows], high[:, cols], TN)
                term += mul(high[:, rows], low[:, cols], TN)
                a[b : b + BLOCK, b:] -= term + mul(low[:, rows], high[:, cols], TN)

    @pl.when(p == last)
    def _():
        share = mine_ref.shape[0]
        top = pl.multiple_of(place_ref[0] * share, share)
        below = lax.broadcasted_iota(jnp.int32, mine_ref.shape, 0) + top
        cols = lax.broadcasted_iota(jnp.int32, mine_ref.shape, 1)
        mine_ref[...] = jnp.where(cols >= below, u[pl.ds(top, share), :], 0.0)
        for q in range(HALF // PANEL, last):
            s = (q + 1) * PANEL
            u[s:, q * PANEL : s] = jnp.zeros((ORDER - s, PANEL), F32)
        fetch.wait()
        lead = mul(start_ref[...], u[HALF:, HALF:], TN, EXACT)
        basis = lead / jnp.sqrt(jnp.sum(lead * lead))
        inner = mul(basis, basis, NT, EXACT)
        states = inner.shape[0]
        eye = jnp.where(
            lax.broadcasted_iota(jnp.int32, (states, states), 0)
            == lax.broadcasted_iota(jnp.int32, (states, states), 1),
            1.5,
            0.0,
        ).astype(F32)
        total = None
        for step in range(NSTEPS):
            m = eye - 0.5 * inner
            total = m if total is None else mul(total, m, NN, EXACT)
            if step < NSTEPS - 1:
                inner = mul(mul(inner, m, NN, EXACT), m, NN, EXACT)
        basis_ref[...] = mul(total, basis, NN, EXACT)


def factor_and_basis(place, own, other, start, share):
    whole = lambda shape: pl.BlockSpec(shape, lambda i: (0,) * len(shape))
    states = start.shape[1]
    return pl.pallas_call(
        factor_kernel,
        grid=(ORDER // PANEL,),
        out_shape=(
            jax.ShapeDtypeStruct((share, ORDER), F32),
            jax.ShapeDtypeStruct((states, HALF), F32),
        ),
        in_specs=[SMEM, whole(own.shape), whole(other.shape), HBM],
        out_specs=(whole((share, ORDER)), whole((states, HALF))),
        scratch_shapes=[
            pltpu.VMEM((ORDER, ORDER), F32),
            pltpu.VMEM((ORDER, ORDER), F32),
            pltpu.VMEM((PANEL, PANEL), F32),
            pltpu.VMEM(start.shape, F32),
            pltpu.SemaphoreType.DMA((1,)),
        ],
        compiler_params=params(32),
        name="factor",
    )(place, own, other, pltpu.with_memory_space_constraint(start, pltpu.HBM))


def states_kernel(basis_ref, x_ref, out_ref, high_ref, low_ref):
    span = out_ref.shape[1]
    start = pl.multiple_of(pl.program_id(0) * span, span)
    window = x_ref[:, pl.ds(start, span + PAD)]
    first = BR // 2
    for k in range(first):
        high, low = split(window[:, first + k : first + k + span])
        high_ref[k * CH : (k + 1) * CH, :] = high
        low_ref[k * CH : (k + 1) * CH, :] = low
    bh, bl = split(basis_ref[...])
    out = mul(bh, high_ref[...], NN)
    out += mul(bl, high_ref[...], NN)
    out_ref[...] = out + mul(bh, low_ref[...], NN)


def project(basis, x):
    states = basis.shape[0]
    count = x.shape[1] - PAD
    span = 2048
    slab = pltpu.VMEM((HALF, span), BF16)
    return pl.pallas_call(
        states_kernel,
        grid=(count // span,),
        out_shape=jax.ShapeDtypeStruct((states, count), F32),
        in_specs=[
            pl.BlockSpec(basis.shape, lambda i: (0, 0)),
            pl.BlockSpec(x.shape, lambda i: (0, 0)),
        ],
        out_specs=pl.BlockSpec((states, span), lambda i: (0, i)),
        scratch_shapes=[slab, slab],
        compiler_params=params(32),
        name="states",
    )(basis, x)


def windows(samples, halo, first, width, nearest):
    chans, chan = lax.axis_size("chan"), lax.axis_index("chan")
    count = samples.shape[1] // chans
    owed = []
    for away in range(nearest, chans):
        to = (chan + away) % chans
        window = lax.dynamic_slice_in_dim(samples, to * count + first, width, 1)
        if halo is not None:
            end = jnp.minimum((to + 1) * count, samples.shape[1] - PAD)
            tail = lax.dynamic_slice_in_dim(samples, end, PAD, 1)
            window = jnp.concatenate([window, jnp.where(to == chans - 1, halo, tail)], 1)
        owed.append(window)
    return owed


def exchange(owed):
    chans = lax.axis_size("chan")
    return [
        lax.ppermute(window, "chan", [(i, (i + away) % chans) for i in range(chans)])
        for away, window in enumerate(owed, 1)
    ]


def per_device(samples, start_basis):
    times, chans = lax.axis_size(TIME), lax.axis_size("chan")
    count = samples.shape[1] // chans
    core = lax.axis_index("core")
    place = jnp.stack([lax.axis_index("chan"), core]).astype(jnp.int32)
    halo = lax.ppermute(samples[:, :PAD], TIME, [(i, i - 1) for i in range(1, times)])
    own, *owed = windows(samples, None, 0, CHUNK + PAD, 0)
    pieces = [own] + exchange(owed)
    own, *owed = windows(samples, halo, CHUNK, count - CHUNK, 0)
    others = [own] + exchange(owed)
    before = gram_chunk(place, pieces)
    x, keep, send = gram_chunk(place, others, before)
    swap = [(0, 1), (1, 0)]
    half = keep + lax.ppermute(send, "core", swap)
    half = lax.all_to_all(half, CHIPS, 0, 0, tiled=True)
    half = jnp.broadcast_to(jnp.sum(half, 0)[None], half.shape)
    half = lax.all_to_all(half, CHIPS, 0, 0, tiled=True)
    other = lax.ppermute(half, "core", swap)
    place = jnp.stack([lax.axis_index(ALL), core]).astype(jnp.int32)
    mine, basis = factor_and_basis(place, half, other, start_basis, ORDER // (times * chans))
    return (mine, project(basis, x))


def solution(mesh):
    mesh = Mesh(mesh.devices.reshape(4, 4, 2, 4), ALL)
    return jax.shard_map(
        per_device,
        mesh=mesh,
        in_specs=(P("chan", TIME), P()),
        out_specs=(P(ALL, None), P(None, ALL)),
        check_vma=False,
    )
```

```python
import functools

import jax
import jax.numpy as jnp
from jax import lax
from jax.experimental import pallas as pl
from jax.experimental.pallas import tpu as pltpu
from jax.sharding import Mesh
from jax.sharding import PartitionSpec as P

BR = 16
NSTEPS = 6
CH = 64
ORDER = 1024
HALF = 512
PANEL = 128
BLOCK = 256
PAD = 128
STEP = 512
CHUNK = 2048
EARLY = 1664
TILES = 640
F32 = jnp.float32
BF16 = jnp.bfloat16
ALL = ("x", "y", "core", "chan")
TIME = ("x", "y", "core")
CHIPS = ("x", "y", "chan")
NN = (((1,), (0,)), ((), ()))
NT = (((1,), (1,)), ((), ()))
TN = (((0,), (0,)), ((), ()))
VMEM = pl.BlockSpec(memory_space=pltpu.VMEM)
SMEM = pl.BlockSpec(memory_space=pltpu.SMEM)
HBM = pl.BlockSpec(memory_space=pltpu.HBM)


def params(mebibytes):
    return pltpu.CompilerParams(vmem_limit_bytes=mebibytes << 20)


def mul(left, right, dims, precision=None):
    return lax.dot_general(
        left, right, dims, precision=precision, preferred_element_type=F32
    )


def mul3(left, right, dims):
    (lh, ll), (rh, rl) = split(left), split(right)
    return mul(lh, rh, dims) + mul(lh, rl, dims) + mul(ll, rh, dims)


def upper_tiles():
    for top in range(0, ORDER, BLOCK):
        for row in range(top, top + BLOCK, 8):
            for col in range(top, ORDER, 128):
                yield row, col


def split(value):
    high = value.astype(BF16)
    return high, (value - high.astype(F32)).astype(BF16)


def gram_kernel(size, start, place_ref, p0_ref, p1_ref, p2_ref, p3_ref, *refs):
    group = CH // 4
    pieces = (p0_ref, p1_ref, p2_ref, p3_ref)
    strips = [
        pl.ds(pl.multiple_of((place_ref[0] + 4 - away) % 4 * group, group), group) for away in range(4)
    ]
    bulk = []
    if start is None:
        x_ref, g, cross, h0, l0, h1, l1 = refs
        base = 0
        g[...] = jnp.zeros_like(g)
        cross[...] = jnp.zeros_like(cross)
        for strip, piece in zip(strips, pieces):
            x_ref[strip, :] = piece[...]
    else:
        before_ref, sofar_ref, mixed_ref, *refs = refs
        x_ref, keep_ref, send_ref, h0, l0, h1, l1, g, cross, sems = refs
        base = start
        early = []
        for part, first, count, into in ((0, 0, EARLY, early), (1, EARLY, size + PAD - EARLY, bulk)):
            for away, (strip, piece) in enumerate(zip(strips, pieces)):
                to = x_ref.at[strip, pl.ds(base + first, count)]
                into.append(
                    pltpu.make_async_copy(piece.at[:, pl.ds(first, count)], to, sems.at[part, away])
                )
        for copy in early + bulk:
            copy.start()
        g[...] = sofar_ref[...]
        cross[...] = mixed_ref[...]
        x_ref[:, :start] = before_ref[:, :start]
        for copy in early:
            copy.wait()

    def prepare(at, high_ref, low_ref):
        window = x_ref[:, pl.ds(at, STEP + PAD)]
        first = window[:, :STEP]
        root = lax.rsqrt(1.0 + jnp.sum(first * first, 0, keepdims=True) * (1.0 / CH))
        for k in range(BR):
            high, low = split(window[:, k : k + STEP] * root)
            high_ref[k * CH : (k + 1) * CH, :] = high
            low_ref[k * CH : (k + 1) * CH, :] = low

    def accumulate(high_ref, low_ref):
        for index, top in enumerate(range(0, ORDER, BLOCK)):
            end = top + BLOCK
            rows, cols = slice(top, end), slice(top, ORDER)
            both = mul(high_ref[rows, :], high_ref[cols, :], NT)
            mixed = mul(high_ref[rows, :], low_ref[cols, :], NT)
            g[rows, rows] += both[:, :BLOCK]
            cross[index] += mixed[:, :BLOCK]
            if end < ORDER:
                rest = slice(end, ORDER)
                other = mul(low_ref[rows, :], high_ref[rest, :], NT)
                g[rows, rest] += both[:, BLOCK:] + mixed[:, BLOCK:] + other

    prepare(base, h0, l0)

    def pair(j, carry):
        at = base + j * (2 * STEP)
        if bulk:

            @pl.when(j == 1)
            def _():
                for copy in bulk:
                    copy.wait()

        prepare(pl.multiple_of(at + STEP, STEP), h1, l1)
        accumulate(h0, l0)
        after = jnp.minimum(at + 2 * STEP, base + size - STEP)
        prepare(pl.multiple_of(after, STEP), h0, l0)
        accumulate(h1, l1)
        return carry

    lax.fori_loop(0, size // (2 * STEP), pair, 0)
    if start is None:
        return
    for index, top in enumerate(range(0, ORDER, BLOCK)):
        rows = slice(top, top + BLOCK)
        g[rows, rows] += cross[index] + cross[index].T
    scale = 1.0 / ((base + size) * 128)
    for core in range(2):

        @pl.when(place_ref[1] == core)
        def _():
            for tile, (row, col) in enumerate(upper_tiles()):
                half, piece, at = where(tile)
                to_ref = keep_ref if half == core else send_ref
                to_ref[piece, at : at + 8, :] = g[row : row + 8, col : col + 128] * scale


def where(tile):
    piece, at = divmod(tile, TILES // 128)
    return piece // 64, piece % 64, 8 * at


def gram_chunk(place, pieces, before=None):
    size = pieces[1].shape[1] - PAD
    slab = pltpu.VMEM((ORDER, STEP), BF16)
    square, blocks = (ORDER, ORDER), (ORDER // BLOCK, BLOCK, BLOCK)
    gram, mixed = jax.ShapeDtypeStruct(square, F32), jax.ShapeDtypeStruct(blocks, F32)
    half = jax.ShapeDtypeStruct((64, 8 * TILES // 128, 128), F32)
    if before is None:
        start, given, into, out, scratch = None, [], VMEM, (gram, mixed), []
    else:
        start, given, into, out = before[0].shape[1] - PAD, list(before), HBM, (half, half)
        pieces = [pltpu.with_memory_space_constraint(piece, pltpu.HBM) for piece in pieces]
        scratch = [pltpu.VMEM(square, F32), pltpu.VMEM(blocks, F32), pltpu.SemaphoreType.DMA((2, 4))]
    x = jax.ShapeDtypeStruct((CH, size + PAD + (start or 0)), F32)
    return pl.pallas_call(
        functools.partial(gram_kernel, size, start),
        out_shape=(x,) + out,
        in_specs=[SMEM] + [into] * 4 + [VMEM] * len(given),
        out_specs=(VMEM,) * 3,
        scratch_shapes=[slab] * 4 + scratch,
        compiler_params=params(32),
        name="gram_first" if start is None else "gram_last",
    )(place, *pieces, *given)


def lane(value, j):
    return jnp.broadcast_to(value[:, j : j + 1], (8, 128))


def row(value, j):
    return jnp.broadcast_to(value[j : j + 1, :], (8, 128))


def diagonal_factor(d):
    n = PANEL // 8
    rows = lax.broadcasted_iota(jnp.int32, (8, 128), 0)
    cols = lax.broadcasted_iota(jnp.int32, (8, 128), 1)
    w = [jnp.where(cols == rows + 8 * i, 1.0, 0.0).astype(F32) for i in range(n)]
    upper, inverse = [], []
    cn = [lane(d[0], j) for j in range(8)]
    for g in range(n):
        cg = cn
        below = range(g + 1, n)
        cb = {i: [lane(d[i], 8 * g + j) for j in range(8)] for i in below}
        if g + 1 < n:
            cn = [lane(d[g + 1], 8 * (g + 1) + k) for k in range(8)]
        dg, wg = d[g], w[g]
        tops, inv = [], []
        pivots = jnp.zeros((8, 128), F32)
        for j in range(8):
            pivot = row(cg[j], j)
            r = 1.0 / pivot
            inv.append(r)
            pivots = jnp.where(rows == j, pivot, pivots)
            under = jnp.where(rows > j, cg[j], 0.0)
            top = {k: row(cg[k], j) for k in range(j + 1, 8)}
            tops.append(top)
            for k in range(j + 1, 8):
                cg[k] = cg[k] - (under * top[k]) * r
            dg = dg - (under * row(dg, j)) * r
            wg = wg - (under * row(wg, j)) * r
        scale = lax.rsqrt(pivots)
        upper.append(jnp.where(cols >= rows + 8 * g, dg * scale, 0.0))
        inverse.append(wg * scale)
        ds = [row(dg, j) for j in range(8)]
        ws = [row(wg, j) for j in range(8)]
        for i in below:
            c, di, wi = cb[i], d[i], w[i]
            for j in range(8):
                m = c[j] * inv[j]
                if i == g + 1:
                    cn = [cn[k] - m * row(c[j], k) for k in range(8)]
                for k in range(j + 1, 8):
                    c[k] = c[k] - m * tops[j][k]
                di = di - m * ds[j]
                wi = wi - m * ws[j]
            d[i], w[i] = di, wi
    return upper, inverse


def factor_kernel(
    place_ref, own_ref, other_ref, given_ref, mine_ref, basis_ref, a, u, inverse_ref, start_ref, sem
):
    p = pl.program_id(0)
    last = ORDER // PANEL - 1
    fetch = pltpu.make_async_copy(given_ref, start_ref, sem.at[0])

    @pl.when(p == 0)
    def _():
        fetch.start()
        for core in range(2):

            @pl.when(place_ref[1] == core)
            def _():
                for tile, (r, c) in enumerate(upper_tiles()):
                    half, piece, at = where(tile)
                    from_ref = own_ref if half == core else other_ref
                    a[r : r + 8, c : c + 128] = from_ref[piece, at : at + 8, :]

    o = pl.multiple_of(p * PANEL, PANEL)
    strips = [pl.ds(pl.multiple_of(o + 8 * i, 8), 8) for i in range(PANEL // 8)]
    upper, inverse = diagonal_factor([a[s, pl.ds(o, PANEL)] for s in strips])
    for i, s in enumerate(strips):
        u[s, pl.ds(o, PANEL)] = upper[i]
        inverse_ref[8 * i : 8 * i + 8, :] = inverse[i]
    for q in range(ORDER // PANEL - 1):

        @pl.when(p == q)
        def _():
            top, s = q * PANEL, (q + 1) * PANEL
            panel = mul3(inverse_ref[...], a[top:s, s:], NN)
            u[top:s, s:] = panel
            high, low = split(panel)
            for b in range(s, ORDER, BLOCK):
                rows, cols = slice(b - s, min(b + BLOCK, ORDER) - s), slice(b - s, ORDER - s)
                term = mul(high[:, rows], high[:, cols], TN)
                term += mul(high[:, rows], low[:, cols], TN)
                a[b : b + BLOCK, b:] -= term + mul(low[:, rows], high[:, cols], TN)

    @pl.when(p == last)
    def _():
        share = mine_ref.shape[0]
        top = pl.multiple_of(place_ref[0] * share, share)
        below = lax.broadcasted_iota(jnp.int32, mine_ref.shape, 0) + top
        cols = lax.broadcasted_iota(jnp.int32, mine_ref.shape, 1)
        mine_ref[...] = jnp.where(cols >= below, u[pl.ds(top, share), :], 0.0)
        for q in range(HALF // PANEL, last):
            s = (q + 1) * PANEL
            u[s:, q * PANEL : s] = jnp.zeros((ORDER - s, PANEL), F32)
        fetch.wait()
        lead = mul3(start_ref[...], u[HALF:, HALF:], TN)
        basis = lead / jnp.sqrt(jnp.sum(lead * lead))
        inner = mul3(basis, basis, NT)
        states = inner.shape[0]
        eye = jnp.where(
            lax.broadcasted_iota(jnp.int32, (states, states), 0)
            == lax.broadcasted_iota(jnp.int32, (states, states), 1),
            1.5,
            0.0,
        ).astype(F32)
        total = None
        for step in range(NSTEPS):
            m = eye - 0.5 * inner
            total = m if total is None else mul3(total, m, NN)
            if step < NSTEPS - 1:
                inner = mul3(mul3(inner, m, NN), m, NN)
        basis_ref[...] = mul3(total, basis, NN)


def factor_and_basis(place, own, other, start, share):
    whole = lambda shape: pl.BlockSpec(shape, lambda i: (0,) * len(shape))
    states = start.shape[1]
    return pl.pallas_call(
        factor_kernel,
        grid=(ORDER // PANEL,),
        out_shape=(
            jax.ShapeDtypeStruct((share, ORDER), F32),
            jax.ShapeDtypeStruct((states, HALF), F32),
        ),
        in_specs=[SMEM, whole(own.shape), whole(other.shape), HBM],
        out_specs=(whole((share, ORDER)), whole((states, HALF))),
        scratch_shapes=[
            pltpu.VMEM((ORDER, ORDER), F32),
            pltpu.VMEM((ORDER, ORDER), F32),
            pltpu.VMEM((PANEL, PANEL), F32),
            pltpu.VMEM(start.shape, F32),
            pltpu.SemaphoreType.DMA((1,)),
        ],
        compiler_params=params(32),
        name="factor",
    )(place, own, other, pltpu.with_memory_space_constraint(start, pltpu.HBM))


def states_kernel(basis_ref, x_ref, out_ref, high_ref, low_ref):
    span = out_ref.shape[1]
    start = pl.multiple_of(pl.program_id(0) * span, span)
    window = x_ref[:, pl.ds(start, span + PAD)]
    first = BR // 2
    for k in range(first):
        high, low = split(window[:, first + k : first + k + span])
        high_ref[k * CH : (k + 1) * CH, :] = high
        low_ref[k * CH : (k + 1) * CH, :] = low
    bh, bl = split(basis_ref[...])
    out = mul(bh, high_ref[...], NN)
    out += mul(bl, high_ref[...], NN)
    out_ref[...] = out + mul(bh, low_ref[...], NN)


def project(basis, x):
    states = basis.shape[0]
    count = x.shape[1] - PAD
    span = 4096
    slab = pltpu.VMEM((HALF, span), BF16)
    return pl.pallas_call(
        states_kernel,
        grid=(count // span,),
        out_shape=jax.ShapeDtypeStruct((states, count), F32),
        in_specs=[
            pl.BlockSpec(basis.shape, lambda i: (0, 0)),
            pl.BlockSpec(x.shape, lambda i: (0, 0)),
        ],
        out_specs=pl.BlockSpec((states, span), lambda i: (0, i)),
        scratch_shapes=[slab, slab],
        compiler_params=params(32),
        name="states",
    )(basis, x)


def windows(samples, halo, first, width, nearest):
    chans, chan = lax.axis_size("chan"), lax.axis_index("chan")
    count = samples.shape[1] // chans
    owed = []
    for away in range(nearest, chans):
        to = (chan + away) % chans
        window = lax.dynamic_slice_in_dim(samples, to * count + first, width, 1)
        if halo is not None:
            end = jnp.minimum((to + 1) * count, samples.shape[1] - PAD)
            tail = lax.dynamic_slice_in_dim(samples, end, PAD, 1)
            window = jnp.concatenate([window, jnp.where(to == chans - 1, halo, tail)], 1)
        owed.append(window)
    return owed


def exchange(owed):
    chans = lax.axis_size("chan")
    return [
        lax.ppermute(window, "chan", [(i, (i + away) % chans) for i in range(chans)])
        for away, window in enumerate(owed, 1)
    ]


def per_device(samples, start_basis):
    times, chans = lax.axis_size(TIME), lax.axis_size("chan")
    count = samples.shape[1] // chans
    core = lax.axis_index("core")
    place = jnp.stack([lax.axis_index("chan"), core]).astype(jnp.int32)
    halo = lax.ppermute(samples[:, :PAD], TIME, [(i, i - 1) for i in range(1, times)])
    own, *owed = windows(samples, None, 0, CHUNK + PAD, 0)
    pieces = [own] + exchange(owed)
    own, *owed = windows(samples, halo, CHUNK, count - CHUNK, 0)
    others = [own] + exchange(owed)
    before = gram_chunk(place, pieces)
    x, keep, send = gram_chunk(place, others, before)
    swap = [(0, 1), (1, 0)]
    half = keep + lax.ppermute(send, "core", swap)
    half = lax.all_to_all(half, CHIPS, 0, 0, tiled=True)
    half = jnp.broadcast_to(jnp.sum(half, 0)[None], half.shape)
    half = lax.all_to_all(half, CHIPS, 0, 0, tiled=True)
    other = lax.ppermute(half, "core", swap)
    place = jnp.stack([lax.axis_index(ALL), core]).astype(jnp.int32)
    mine, basis = factor_and_basis(place, half, other, start_basis, ORDER // (times * chans))
    return (mine, project(basis, x))


def solution(mesh):
    mesh = Mesh(mesh.devices.reshape(4, 4, 2, 4), ALL)
    return jax.shard_map(
        per_device,
        mesh=mesh,
        in_specs=(P("chan", TIME), P()),
        out_specs=(P(ALL, None), P(None, ALL)),
        check_vma=False,
    )
```

```python
import functools

import jax
import jax.numpy as jnp
from jax import lax
from jax.experimental import pallas as pl
from jax.experimental.pallas import tpu as pltpu
from jax.sharding import Mesh
from jax.sharding import PartitionSpec as P

BR = 16
NSTEPS = 6
CH = 64
ORDER = 1024
HALF = 512
PANEL = 128
BLOCK = 256
PAD = 128
STEP = 512
CHUNK = 2048
EARLY = 1664
TILES = 640
F32 = jnp.float32
BF16 = jnp.bfloat16
ALL = ("x", "y", "core", "chan")
TIME = ("x", "y", "core")
CHIPS = ("y", "chan", "x")
NN = (((1,), (0,)), ((), ()))
NT = (((1,), (1,)), ((), ()))
TN = (((0,), (0,)), ((), ()))
VMEM = pl.BlockSpec(memory_space=pltpu.VMEM)
SMEM = pl.BlockSpec(memory_space=pltpu.SMEM)
HBM = pl.BlockSpec(memory_space=pltpu.HBM)


def params(mebibytes):
    return pltpu.CompilerParams(vmem_limit_bytes=mebibytes << 20)


def mul(left, right, dims, precision=None):
    return lax.dot_general(
        left, right, dims, precision=precision, preferred_element_type=F32
    )


def mul3(left, right, dims):
    (lh, ll), (rh, rl) = split(left), split(right)
    return mul(lh, rh, dims) + mul(lh, rl, dims) + mul(ll, rh, dims)


def upper_tiles():
    for top in range(0, ORDER, BLOCK):
        for row in range(top, top + BLOCK, 8):
            for col in range(top, ORDER, 128):
                yield row, col


def split(value):
    high = value.astype(BF16)
    return high, (value - high.astype(F32)).astype(BF16)


def gram_kernel(size, start, place_ref, p0_ref, p1_ref, p2_ref, p3_ref, *refs):
    group = CH // 4
    pieces = (p0_ref, p1_ref, p2_ref, p3_ref)
    strips = [
        pl.ds(pl.multiple_of((place_ref[0] + 4 - away) % 4 * group, group), group) for away in range(4)
    ]
    bulk = []
    if start is None:
        x_ref, g, cross, h0, l0, h1, l1 = refs
        base = 0
        g[...] = jnp.zeros_like(g)
        cross[...] = jnp.zeros_like(cross)
        for strip, piece in zip(strips, pieces):
            x_ref[strip, :] = piece[...]
    else:
        before_ref, sofar_ref, mixed_ref, *refs = refs
        x_ref, keep_ref, send_ref, h0, l0, h1, l1, g, cross, sems = refs
        base = start
        early = []
        for part, first, count, into in ((0, 0, EARLY, early), (1, EARLY, size + PAD - EARLY, bulk)):
            for away, (strip, piece) in enumerate(zip(strips, pieces)):
                to = x_ref.at[strip, pl.ds(base + first, count)]
                into.append(
                    pltpu.make_async_copy(piece.at[:, pl.ds(first, count)], to, sems.at[part, away])
                )
        for copy in early + bulk:
            copy.start()
        g[...] = sofar_ref[...]
        cross[...] = mixed_ref[...]
        x_ref[:, :start] = before_ref[:, :start]
        for copy in early:
            copy.wait()

    def prepare(at, high_ref, low_ref):
        window = x_ref[:, pl.ds(at, STEP + PAD)]
        first = window[:, :STEP]
        root = lax.rsqrt(1.0 + jnp.sum(first * first, 0, keepdims=True) * (1.0 / CH))
        for k in range(BR):
            high, low = split(window[:, k : k + STEP] * root)
            high_ref[k * CH : (k + 1) * CH, :] = high
            low_ref[k * CH : (k + 1) * CH, :] = low

    def accumulate(high_ref, low_ref):
        for index, top in enumerate(range(0, ORDER, BLOCK)):
            end = top + BLOCK
            rows, cols = slice(top, end), slice(top, ORDER)
            both = mul(high_ref[rows, :], high_ref[cols, :], NT)
            mixed = mul(high_ref[rows, :], low_ref[cols, :], NT)
            g[rows, rows] += both[:, :BLOCK]
            cross[index] += mixed[:, :BLOCK]
            if end < ORDER:
                rest = slice(end, ORDER)
                other = mul(low_ref[rows, :], high_ref[rest, :], NT)
                g[rows, rest] += both[:, BLOCK:] + mixed[:, BLOCK:] + other

    prepare(base, h0, l0)

    def pair(j, carry):
        at = base + j * (2 * STEP)
        if bulk:

            @pl.when(j == 1)
            def _():
                for copy in bulk:
                    copy.wait()

        prepare(pl.multiple_of(at + STEP, STEP), h1, l1)
        accumulate(h0, l0)
        after = jnp.minimum(at + 2 * STEP, base + size - STEP)
        prepare(pl.multiple_of(after, STEP), h0, l0)
        accumulate(h1, l1)
        return carry

    lax.fori_loop(0, size // (2 * STEP), pair, 0)
    if start is None:
        return
    for index, top in enumerate(range(0, ORDER, BLOCK)):
        rows = slice(top, top + BLOCK)
        g[rows, rows] += cross[index] + cross[index].T
    scale = 1.0 / ((base + size) * 128)
    for core in range(2):

        @pl.when(place_ref[1] == core)
        def _():
            for tile, (row, col) in enumerate(upper_tiles()):
                half, piece, at = where(tile)
                to_ref = keep_ref if half == core else send_ref
                to_ref[piece, at : at + 8, :] = g[row : row + 8, col : col + 128] * scale


def where(tile):
    piece, at = divmod(tile, TILES // 128)
    return piece // 64, piece % 64, 8 * at


def gram_chunk(place, pieces, before=None):
    size = pieces[1].shape[1] - PAD
    slab = pltpu.VMEM((ORDER, STEP), BF16)
    square, blocks = (ORDER, ORDER), (ORDER // BLOCK, BLOCK, BLOCK)
    gram, mixed = jax.ShapeDtypeStruct(square, F32), jax.ShapeDtypeStruct(blocks, F32)
    half = jax.ShapeDtypeStruct((64, 8 * TILES // 128, 128), F32)
    if before is None:
        start, given, into, out, scratch = None, [], VMEM, (gram, mixed), []
    else:
        start, given, into, out = before[0].shape[1] - PAD, list(before), HBM, (half, half)
        pieces = [pltpu.with_memory_space_constraint(piece, pltpu.HBM) for piece in pieces]
        scratch = [pltpu.VMEM(square, F32), pltpu.VMEM(blocks, F32), pltpu.SemaphoreType.DMA((2, 4))]
    x = jax.ShapeDtypeStruct((CH, size + PAD + (start or 0)), F32)
    return pl.pallas_call(
        functools.partial(gram_kernel, size, start),
        out_shape=(x,) + out,
        in_specs=[SMEM] + [into] * 4 + [VMEM] * len(given),
        out_specs=(VMEM,) * 3,
        scratch_shapes=[slab] * 4 + scratch,
        compiler_params=params(32),
        name="gram_first" if start is None else "gram_last",
    )(place, *pieces, *given)


def lane(value, j):
    return jnp.broadcast_to(value[:, j : j + 1], (8, 128))


def row(value, j):
    return jnp.broadcast_to(value[j : j + 1, :], (8, 128))


def diagonal_factor(d):
    n = PANEL // 8
    rows = lax.broadcasted_iota(jnp.int32, (8, 128), 0)
    cols = lax.broadcasted_iota(jnp.int32, (8, 128), 1)
    w = [jnp.where(cols == rows + 8 * i, 1.0, 0.0).astype(F32) for i in range(n)]
    upper, inverse = [], []
    cn = [lane(d[0], j) for j in range(8)]
    for g in range(n):
        cg = cn
        below = range(g + 1, n)
        cb = {i: [lane(d[i], 8 * g + j) for j in range(8)] for i in below}
        if g + 1 < n:
            cn = [lane(d[g + 1], 8 * (g + 1) + k) for k in range(8)]
        dg, wg = d[g], w[g]
        tops, inv = [], []
        pivots = jnp.zeros((8, 128), F32)
        for j in range(8):
            pivot = row(cg[j], j)
            r = 1.0 / pivot
            inv.append(r)
            pivots = jnp.where(rows == j, pivot, pivots)
            under = jnp.where(rows > j, cg[j], 0.0)
            top = {k: row(cg[k], j) for k in range(j + 1, 8)}
            tops.append(top)
            for k in range(j + 1, 8):
                cg[k] = cg[k] - (under * top[k]) * r
            dg = dg - (under * row(dg, j)) * r
            wg = wg - (under * row(wg, j)) * r
        scale = lax.rsqrt(pivots)
        upper.append(jnp.where(cols >= rows + 8 * g, dg * scale, 0.0))
        inverse.append(wg * scale)
        ds = [row(dg, j) for j in range(8)]
        ws = [row(wg, j) for j in range(8)]
        for i in below:
            c, di, wi = cb[i], d[i], w[i]
            for j in range(8):
                m = c[j] * inv[j]
                if i == g + 1:
                    cn = [cn[k] - m * row(c[j], k) for k in range(8)]
                for k in range(j + 1, 8):
                    c[k] = c[k] - m * tops[j][k]
                di = di - m * ds[j]
                wi = wi - m * ws[j]
            d[i], w[i] = di, wi
    return upper, inverse


def factor_kernel(
    place_ref, own_ref, other_ref, given_ref, mine_ref, basis_ref, a, u, inverse_ref, start_ref, sem
):
    p = pl.program_id(0)
    last = ORDER // PANEL - 1
    fetch = pltpu.make_async_copy(given_ref, start_ref, sem.at[0])

    @pl.when(p == 0)
    def _():
        fetch.start()
        for core in range(2):

            @pl.when(place_ref[1] == core)
            def _():
                for tile, (r, c) in enumerate(upper_tiles()):
                    half, piece, at = where(tile)
                    from_ref = own_ref if half == core else other_ref
                    a[r : r + 8, c : c + 128] = from_ref[piece, at : at + 8, :]

    o = pl.multiple_of(p * PANEL, PANEL)
    strips = [pl.ds(pl.multiple_of(o + 8 * i, 8), 8) for i in range(PANEL // 8)]
    upper, inverse = diagonal_factor([a[s, pl.ds(o, PANEL)] for s in strips])
    for i, s in enumerate(strips):
        u[s, pl.ds(o, PANEL)] = upper[i]
        inverse_ref[8 * i : 8 * i + 8, :] = inverse[i]
    for q in range(ORDER // PANEL - 1):

        @pl.when(p == q)
        def _():
            top, s = q * PANEL, (q + 1) * PANEL
            panel = mul3(inverse_ref[...], a[top:s, s:], NN)
            u[top:s, s:] = panel
            high, low = split(panel)
            for b in range(s, ORDER, BLOCK):
                rows, cols = slice(b - s, min(b + BLOCK, ORDER) - s), slice(b - s, ORDER - s)
                term = mul(high[:, rows], high[:, cols], TN)
                term += mul(high[:, rows], low[:, cols], TN)
                a[b : b + BLOCK, b:] -= term + mul(low[:, rows], high[:, cols], TN)

    @pl.when(p == last)
    def _():
        share = mine_ref.shape[0]
        top = pl.multiple_of(place_ref[0] * share, share)
        below = lax.broadcasted_iota(jnp.int32, mine_ref.shape, 0) + top
        cols = lax.broadcasted_iota(jnp.int32, mine_ref.shape, 1)
        mine_ref[...] = jnp.where(cols >= below, u[pl.ds(top, share), :], 0.0)
        for q in range(HALF // PANEL, last):
            s = (q + 1) * PANEL
            u[s:, q * PANEL : s] = jnp.zeros((ORDER - s, PANEL), F32)
        fetch.wait()
        lead = mul3(start_ref[...], u[HALF:, HALF:], TN)
        basis = lead / jnp.sqrt(jnp.sum(lead * lead))
        inner = mul3(basis, basis, NT)
        states = inner.shape[0]
        eye = jnp.where(
            lax.broadcasted_iota(jnp.int32, (states, states), 0)
            == lax.broadcasted_iota(jnp.int32, (states, states), 1),
            1.5,
            0.0,
        ).astype(F32)
        total = None
        for step in range(NSTEPS):
            m = eye - 0.5 * inner
            total = m if total is None else mul3(total, m, NN)
            if step < NSTEPS - 1:
                inner = mul3(mul3(inner, m, NN), m, NN)
        basis_ref[...] = mul3(total, basis, NN)


def factor_and_basis(place, own, other, start, share):
    whole = lambda shape: pl.BlockSpec(shape, lambda i: (0,) * len(shape))
    states = start.shape[1]
    return pl.pallas_call(
        factor_kernel,
        grid=(ORDER // PANEL,),
        out_shape=(
            jax.ShapeDtypeStruct((share, ORDER), F32),
            jax.ShapeDtypeStruct((states, HALF), F32),
        ),
        in_specs=[SMEM, whole(own.shape), whole(other.shape), HBM],
        out_specs=(whole((share, ORDER)), whole((states, HALF))),
        scratch_shapes=[
            pltpu.VMEM((ORDER, ORDER), F32),
            pltpu.VMEM((ORDER, ORDER), F32),
            pltpu.VMEM((PANEL, PANEL), F32),
            pltpu.VMEM(start.shape, F32),
            pltpu.SemaphoreType.DMA((1,)),
        ],
        compiler_params=params(32),
        name="factor",
    )(place, own, other, pltpu.with_memory_space_constraint(start, pltpu.HBM))


def states_kernel(basis_ref, x_ref, out_ref, high_ref, low_ref):
    span = out_ref.shape[1]
    start = pl.multiple_of(pl.program_id(0) * span, span)
    window = x_ref[:, pl.ds(start, span + PAD)]
    first = BR // 2
    for k in range(first):
        high, low = split(window[:, first + k : first + k + span])
        high_ref[k * CH : (k + 1) * CH, :] = high
        low_ref[k * CH : (k + 1) * CH, :] = low
    bh, bl = split(basis_ref[...])
    out = mul(bh, high_ref[...], NN)
    out += mul(bl, high_ref[...], NN)
    out_ref[...] = out + mul(bh, low_ref[...], NN)


def project(basis, x):
    states = basis.shape[0]
    count = x.shape[1] - PAD
    span = 4096
    slab = pltpu.VMEM((HALF, span), BF16)
    return pl.pallas_call(
        states_kernel,
        grid=(count // span,),
        out_shape=jax.ShapeDtypeStruct((states, count), F32),
        in_specs=[
            pl.BlockSpec(basis.shape, lambda i: (0, 0)),
            pl.BlockSpec(x.shape, lambda i: (0, 0)),
        ],
        out_specs=pl.BlockSpec((states, span), lambda i: (0, i)),
        scratch_shapes=[slab, slab],
        compiler_params=params(32),
        name="states",
    )(basis, x)


def windows(samples, halo, first, width, nearest):
    chans, chan = lax.axis_size("chan"), lax.axis_index("chan")
    count = samples.shape[1] // chans
    owed = []
    for away in range(nearest, chans):
        to = (chan + away) % chans
        window = lax.dynamic_slice_in_dim(samples, to * count + first, width, 1)
        if halo is not None:
            end = jnp.minimum((to + 1) * count, samples.shape[1] - PAD)
            tail = lax.dynamic_slice_in_dim(samples, end, PAD, 1)
            window = jnp.concatenate([window, jnp.where(to == chans - 1, halo, tail)], 1)
        owed.append(window)
    return owed


def exchange(owed):
    chans = lax.axis_size("chan")
    return [
        lax.ppermute(window, "chan", [(i, (i + away) % chans) for i in range(chans)])
        for away, window in enumerate(owed, 1)
    ]


def per_device(samples, start_basis):
    times, chans = lax.axis_size(TIME), lax.axis_size("chan")
    count = samples.shape[1] // chans
    core = lax.axis_index("core")
    place = jnp.stack([lax.axis_index("chan"), core]).astype(jnp.int32)
    halo = lax.ppermute(samples[:, :PAD], TIME, [(i, i - 1) for i in range(1, times)])
    own, *owed = windows(samples, None, 0, CHUNK + PAD, 0)
    pieces = [own] + exchange(owed)
    own, *owed = windows(samples, halo, CHUNK, count - CHUNK, 0)
    others = [own] + exchange(owed)
    before = gram_chunk(place, pieces)
    x, keep, send = gram_chunk(place, others, before)
    swap = [(0, 1), (1, 0)]
    half = keep + lax.ppermute(send, "core", swap)
    half = lax.all_to_all(half, CHIPS, 0, 0, tiled=True)
    half = jnp.broadcast_to(jnp.sum(half, 0)[None], half.shape)
    half = lax.all_to_all(half, CHIPS, 0, 0, tiled=True)
    other = lax.ppermute(half, "core", swap)
    place = jnp.stack([lax.axis_index(ALL), core]).astype(jnp.int32)
    mine, basis = factor_and_basis(place, half, other, start_basis, ORDER // (times * chans))
    return (mine, project(basis, x))


def solution(mesh):
    mesh = Mesh(mesh.devices.reshape(4, 4, 2, 4), ALL)
    return jax.shard_map(
        per_device,
        mesh=mesh,
        in_specs=(P("chan", TIME), P()),
        out_specs=(P(ALL, None), P(None, ALL)),
        check_vma=False,
    )
```
